512 devices in a mesh: slab: 16 (over z_hi, x), seq: 32 (over y, z_lo, core).
Axes of the slice: x: 4, y: 4, z: 16 (z_hi: 4, z_lo: 4; z = z_hi * 4 + z_lo), core: 2. Of those that a mesh axis runs over, the one named last changes fastest.
Arguments:
- video_tokens: bfloat16 [512, 512, 1152], P(('slab', 'seq')), may hold values from -40 to 40
- modulation: float32 [512, 3, 1152], P(('slab', 'seq')), may hold values from -3 to 3
- qkv_weight: bfloat16 [1152, 3456], P(None, 'seq'), may hold values from -1.5 to 1.5
- out_weight: bfloat16 [1152, 1152], P(None, 'seq'), may hold values from -0.1875 to 0.1875
Outputs:
- restored: bfloat16 [512, 512, 1152], P(('slab', 'seq'))
The draws below stay inside these ranges and needn't reach their ends.
All inputs are finite; a program needn't handle non-finite values.
Results may differ from the reference program's by a relative error of at most 0.004.
Values may be sent and summed in bfloat16 or wider, within the bound.
A program may use at most 128 MiB of HBM per device.

```python
import jax
import jax.numpy as jnp
from jax import lax

D = 1152
H = 16
HD = 72
FRS = 32
POS_DEV = 16
S = 512
FRAMES = 512
N_SEQ = 32


def draw_video_tokens(key, part):
    key_common = jax.random.fold_in(key, 11)
    values = jax.random.normal(key_common, (FRAMES, S, D), jnp.float32)
    return jnp.clip(values, -40.0, 40.0).astype(jnp.bfloat16)


def draw_qkv_weight(key, part):
    values = jax.random.normal(jax.random.fold_in(key, 21), (D, 3 * D), jnp.float32) * D ** (-0.5)
    return jnp.clip(values, -1.5, 1.5).astype(jnp.bfloat16)


def levels(stream_key, shape, split, smallest, largest):
    level = 1.0
    for position, blocks in split:
        draws = jax.random.uniform(jax.random.fold_in(jax.random.fold_in(stream_key, 6), position), (blocks,), jnp.float32, smallest / len(split), largest / len(split))
        level = level * jnp.repeat(jnp.exp(draws), shape[position] // blocks).reshape((-1,) + (1,) * (len(shape) - 1 - position))
    return level


def noise(own_key, shape, spread, bound, split=(), held_as=jnp.bfloat16):
    entries = spread * jax.random.normal(own_key, shape, jnp.float32)
    if split:
        entries = entries * levels(own_key, shape, split, -0.22, 0.18)
    return jnp.clip(entries, -bound, bound).astype(held_as)


def setup_inputs(seed: int = 0) -> dict:
    splits = jax.random.split(jax.random.key(seed), 5)
    video_tokens = draw_video_tokens(jax.random.fold_in(splits[4], 71), 0)
    modulation = noise(splits[1], (FRAMES, 3, D), 0.5, 3.0, ((0, 512),), jnp.float32)
    qkv_weight = draw_qkv_weight(jax.random.fold_in(splits[4], 71), 0)
    out_weight = noise(splits[3], (D, D), D ** -0.5, 0.1875, ((1, 32),))
    return dict(video_tokens=video_tokens, modulation=modulation, qkv_weight=qkv_weight, out_weight=out_weight)


epsilon = 1e-06

def modulate(tokens, modulation):
    values = tokens.astype(jnp.float32)
    average = lax.optimization_barrier(jnp.mean(values, axis=-1, keepdims=True))
    centered = values - average
    variance = lax.optimization_barrier(jnp.mean(centered * centered, axis=-1, keepdims=True))
    normed = centered * lax.rsqrt(variance + epsilon)
    return (normed * (1.0 + modulation[:, 1][:, None, :]) + modulation[:, 0][:, None, :]).astype(jnp.bfloat16)

def attend(queries, key_rows, value_rows):
    scores = jnp.einsum('wtphd,wsphd->wphts', queries.astype(jnp.float32), key_rows.astype(jnp.float32))
    scores = scores * queries.shape[-1] ** (-0.5)
    scores = scores - lax.optimization_barrier(jnp.max(scores, axis=-1, keepdims=True))
    exponent = jnp.exp(scores)
    softmaxed = (exponent / lax.optimization_barrier(jnp.sum(exponent, axis=-1, keepdims=True))).astype(jnp.bfloat16)
    result = jnp.einsum('wphts,wsphd->wtphd', softmaxed.astype(jnp.float32), value_rows.astype(jnp.float32))
    return result.astype(jnp.bfloat16)

def windows(values):
    return values.reshape(FRAMES // FRS, FRS, values.shape[1], values.shape[2], values.shape[3])

def reference(video_tokens, modulation, qkv_weight, out_weight):
    heads_half = H // 2

    def one_block(block_index):
        offset = (block_index * POS_DEV).astype(jnp.int32)
        tokens = lax.dynamic_slice_in_dim(video_tokens, offset, POS_DEV, 1)
        normed = modulate(tokens, modulation)
        token_rows = normed.reshape(FRAMES * POS_DEV, D)
        projected = jnp.dot(token_rows, qkv_weight, preferred_element_type=jnp.float32).astype(jnp.bfloat16)
        grouped = projected.reshape(FRAMES, POS_DEV, 6, heads_half, HD)
        windowed = attend(windows(grouped[:, :, 0]), windows(grouped[:, :, 1]), windows(grouped[:, :, 2]))
        windowed = windowed.reshape(FRAMES, POS_DEV, heads_half, HD)
        rolled = jnp.roll(grouped[:, :, 3:], FRS // 2, axis=0)
        shifted = attend(windows(rolled[:, :, 0]), windows(rolled[:, :, 1]), windows(rolled[:, :, 2]))
        shifted = jnp.roll(shifted.reshape(FRAMES, POS_DEV, heads_half, HD), -(FRS // 2), axis=0)
        attended = jnp.concatenate([windowed, shifted], axis=2).reshape(FRAMES * POS_DEV, D)
        output_rows = jnp.dot(attended, out_weight, preferred_element_type=jnp.float32).astype(jnp.bfloat16)
        output_rows = output_rows.reshape(FRAMES, POS_DEV, D)
        restored = tokens.astype(jnp.float32) + modulation[:, 2][:, None, :] * output_rows.astype(jnp.float32)
        return restored.astype(jnp.bfloat16)
    blocks_out = lax.map(one_block, jnp.arange(N_SEQ, dtype=jnp.int32))
    return jnp.transpose(blocks_out, (1, 0, 2, 3)).reshape(FRAMES, S, D)
```

```python
import functools

import jax
import jax.numpy as jnp
from jax import lax
from jax.experimental import pallas as pl
from jax.experimental.pallas import tpu as pltpu
from jax.sharding import PartitionSpec as P

D = 1152
HEAD = 72
GROUP = 576
WIDE = 640
NSEQ = 32
NSLAB = 16
QROWS = 108
OROWS = 36
MESH = pl.DeviceIdType.MESH
EPS = 1e-06
BF = jnp.bfloat16
F32 = jnp.float32


def dot_nt(a, b):
    return lax.dot_general(a, b, (((1,), (1,)), ((), ())), preferred_element_type=F32)


def kernel(
    tok_ref, mod_ref, qw_ref, ow_ref, out_ref,
    hbuf, xbuf, wq, wo, wt, wot, xa, xb, halo_l, halo_u,
    qs, kts, vs, att, att_b, edge, ret_l, ret_u, obuf,
    wrecv, zsend, ysend, xsend, ssend, lsem, tsend, trecv, hsem, rsem, osend, orecv,
):
    s = lax.axis_index("slab")
    j = lax.axis_index("seq")
    x = lax.rem(s, 4)
    zh = lax.div(s, 4)
    y = lax.div(j, 8)
    zl = lax.rem(lax.div(j, 2), 4)
    c = lax.rem(j, 2)
    even = lax.rem(x, 2) == 0
    odd = lax.rem(x, 2) == 1
    par = lax.rem(x, 2)

    def zdev(off):
        zz = lax.rem(zh * 4 + zl + off + 16, 16)
        return (lax.div(zz, 4) * 4 + x, y * 8 + lax.rem(zz, 4) * 2 + c)

    def ydev(off):
        return (s, lax.rem(y + off + 4, 4) * 8 + zl * 2 + c)

    def xdev(off):
        return (zh * 4 + lax.rem(x + off + 4, 4), j)

    sib = (s, y * 8 + zl * 2 + (1 - c))
    up = (lax.rem(s + 1, NSLAB), j)
    down = (lax.rem(s + NSLAB - 1, NSLAB), j)

    def rdma(src, dst, ssem, rsem_, dev):
        return pltpu.make_async_remote_copy(
            src_ref=src, dst_ref=dst, send_sem=ssem, recv_sem=rsem_,
            device_id=dev, device_id_type=MESH,
        )

    barrier = pltpu.get_barrier_semaphore()

    def greet(k, carry):
        pl.semaphore_signal(
            barrier, inc=1, device_id=(s, lax.rem(j + k, NSEQ)), device_id_type=MESH
        )
        return carry

    lax.fori_loop(1, NSEQ, greet, 0)
    for dev in (xdev(1), xdev(-1), zdev(1), zdev(-1), zdev(2), zdev(-2), up, down):
        pl.semaphore_signal(barrier, inc=1, device_id=dev, device_id_type=MESH)
    own_q = pltpu.make_async_copy(qw_ref, wq.at[j], lsem.at[0])
    own_o = pltpu.make_async_copy(ow_ref, wo.at[j], lsem.at[1])
    own_q.start()
    own_o.start()
    own_q.wait()
    own_o.wait()
    pl.semaphore_wait(barrier, NSEQ - 1 + 8)

    def slot(yo, zo):
        return lax.rem(y + yo, 4) * 8 + lax.rem(zl + zo, 4) * 2 + c

    def ship(q, sems, i, dev):
        rdma(wq.at[q], wq.at[q], sems.at[0, i], wrecv.at[0, q], dev).start()
        rdma(wo.at[q], wo.at[q], sems.at[1, i], wrecv.at[1, q], dev).start()

    def shipped(sems, i):
        rdma(wq.at[0], wq.at[0], sems.at[0, i], wrecv.at[0, 0], sib).wait_send()
        rdma(wo.at[0], wo.at[0], sems.at[1, i], wrecv.at[1, 0], sib).wait_send()

    def landed(q):
        rdma(wq.at[q], wq.at[q], zsend.at[0, 0], wrecv.at[0, q], sib).wait_recv()
        rdma(wo.at[q], wo.at[q], zsend.at[1, 0], wrecv.at[1, q], sib).wait_recv()

    za = par * 3
    zb = 1 + par
    oa = (1 - par) * 3
    ob = 2 - par
    plus = ((0, 0), (0, 2), (1, 1), (1, 3))

    @pl.when(even)
    def _():
        ship(j, zsend, 0, zdev(-1))

    @pl.when(odd)
    def _():
        ship(j, zsend, 0, zdev(1))
        ship(j, zsend, 1, zdev(-2))

    @pl.when(even)
    def _():
        ship(j, ysend, 0, ydev(1))
        ship(j, ysend, 1, ydev(-1))

    ship(j, ssend, 0, sib)

    shift = mod_ref[0:1, :]
    scale = 1.0 + mod_ref[1:2, :]

    def norm(i, carry):
        rows = pl.ds(pl.multiple_of(i * 32, 32), 32)
        values = tok_ref[rows, :].astype(F32)
        centered = values - jnp.mean(values, axis=-1, keepdims=True)
        variance = jnp.mean(centered * centered, axis=-1, keepdims=True)
        normed = centered * lax.rsqrt(variance + EPS) * scale + shift
        hbuf[pl.ds(i * 2, 2)] = normed.reshape(2, 2, 8, D).astype(BF)
        return carry

    lax.fori_loop(0, 16, norm, 0)

    def send_tokens(k, carry):
        d = lax.rem(j + k, NSEQ)
        rdma(hbuf.at[d], xbuf.at[j], tsend, trecv, (s, d)).start()
        return carry

    lax.fori_loop(1, NSEQ, send_tokens, 0)
    own_tok = pltpu.make_async_copy(hbuf.at[j], xbuf.at[j], lsem.at[2])
    own_tok.start()

    def x_ship(kind, yo, q):
        i = kind * 4 + yo
        ship(q, xsend, i, xdev(1 if (kind, yo) in plus else -1))

    q = slot(0, za)

    @pl.when(odd)
    def _():
        landed(q)
        ship(q, ysend, 0, ydev(1))
        ship(q, ysend, 1, ydev(-1))
        x_ship(0, 0, q)
        ship(q, ssend, 1, sib)

    q1 = slot(0, zb)
    landed(q1)
    ship(q1, ysend, 2, ydev(1))
    ship(q1, ysend, 3, ydev(-1))
    x_ship(1, 0, q1)
    ship(q1, ssend, 2, sib)
    n = 3
    for kind, yo in ((0, 3), (0, 1), (1, 1), (1, 3), (0, 2), (1, 2)):
        q = slot(yo, zb if kind else za)
        landed(q)
        if (kind, yo) == (0, 3):
            ship(q, ysend, 4, ydev(1))
        if (kind, yo) == (1, 1):
            ship(q, ysend, 5, ydev(-1))
        x_ship(kind, yo, q)
        ship(q, ssend, n, sib)
        n += 1

    q0 = slot(0, oa)

    @pl.when(even)
    def _():
        landed(q0)
        ship(q0, ssend, 1, sib)

    for kind, yo in ((1, 0), (0, 1), (0, 3), (1, 1), (1, 3), (0, 2), (1, 2)):
        q = slot(yo, ob if kind else oa)
        landed(q)
        ship(q, ssend, n, sib)
        n += 1

    own_tok.wait()
    rdma(xbuf.at[pl.ds(0, NSEQ - 1)], xbuf.at[pl.ds(0, NSEQ - 1)], tsend, trecv, sib).wait_recv()
    half_up = rdma(xbuf.at[pl.ds(16, 16), 0], halo_l, hsem.at[0], hsem.at[1], up)
    half_down = rdma(xbuf.at[pl.ds(0, 16), 1], halo_u, hsem.at[2], hsem.at[3], down)
    half_up.start()
    half_down.start()

    for b in range(2):
        rows = xbuf[:, b].astype(F32).reshape(256, D).astype(BF)
        xa[256 * b:256 * b + 256, :] = rows
    xb[128:256, :] = xa[0:128, :]
    xb[256:384, :] = xa[384:512, :]

    def other(i, carry):
        landed(i * 2 + 1 - c)
        return carry

    lax.fori_loop(0, 16, other, 0)
    for i in range(16):
        wt[216 * i:216 * i + 216, :] = jnp.concatenate([wq[2 * i], wq[2 * i + 1]], axis=0)
        wot[72 * i:72 * i + 72, :] = jnp.concatenate([wo[2 * i], wo[2 * i + 1]], axis=0)

    def project(g, rows_ref):
        base = 1728 * g
        vbase = 2816 if g else 1152
        rows = rows_ref[...]
        qs[...] = dot_nt(rows, wt[base:base + WIDE, :]).astype(BF)
        kts[...] = dot_nt(wt[base + GROUP:base + GROUP + WIDE, :], rows).astype(BF)
        vs[...] = dot_nt(rows, wt[vbase:vbase + WIDE, :]).astype(BF)

    def attend(g, store):
        phase = 64 * g
        row_id = lax.broadcasted_iota(jnp.int32, (256, 256), 0)
        col_id = lax.broadcasted_iota(jnp.int32, (256, 256), 1)
        same = lax.rem(row_id, 8) == lax.rem(col_id, 8)

        def block(b, carry):
            at = pl.ds(pl.multiple_of(b * 256, 256), 256)
            tiles = {}
            for h in range(8):
                lo = HEAD * h
                t0, t1 = lo // 128, (lo + HEAD - 1) // 128
                width = 128 * (t1 - t0 + 1)
                r = lax.broadcasted_iota(jnp.int32, (width, 256), 0) + t0 * 128
                keep = jnp.where((r >= lo) & (r < lo + HEAD), 1.0, 0.0).astype(BF)
                kt = kts[t0 * 128:t0 * 128 + width, at] * keep
                scores = jnp.dot(
                    qs[at, t0 * 128:t0 * 128 + width], kt, preferred_element_type=F32
                ) * (HEAD ** -0.5)
                scores = jnp.where(same, scores, -1e30)
                top = jnp.max(scores, axis=-1, keepdims=True)
                e = jnp.exp(scores - top)
                p = (e * (1.0 / jnp.sum(e, axis=-1, keepdims=True))).astype(BF)
                lo = HEAD * h + phase
                t0, t1 = lo // 128, (lo + HEAD - 1) // 128
                width = 128 * (t1 - t0 + 1)
                r = lax.broadcasted_iota(jnp.int32, (256, width), 1) + t0 * 128
                keep = jnp.where((r >= lo) & (r < lo + HEAD), 1.0, 0.0).astype(BF)
                v = vs[at, t0 * 128:t0 * 128 + width] * keep
                o = jnp.dot(p, v, preferred_element_type=F32)
                for t in range(t0, t1 + 1):
                    piece = o[:, (t - t0) * 128:(t - t0 + 1) * 128]
                    tiles[t] = tiles[t] + piece if t in tiles else piece
                for t in list(tiles):
                    if h == 7 or t < (HEAD * (h + 1) + phase) // 128:
                        store(at, t, tiles.pop(t).astype(BF))
            return carry

        lax.fori_loop(0, 2, block, 0)

    def store_a(at, t, value):
        if t < 4:
            att[at, t * 128:t * 128 + 128] = value
        else:
            edge[at, :] = value

    def store_b(at, t, value):
        att_b[at, t * 128:t * 128 + 128] = value

    project(0, xa)
    attend(0, store_a)

    half_up.wait()
    half_down.wait()
    xb[0:128, :] = halo_l[...].astype(F32).reshape(128, D).astype(BF)
    xb[384:512, :] = halo_u[...].astype(F32).reshape(128, D).astype(BF)
    project(1, xb)
    attend(1, store_b)

    back_l = rdma(att_b.at[pl.ds(0, 128)], ret_l, rsem.at[0], rsem.at[1], down)
    back_u = rdma(att_b.at[pl.ds(384, 128)], ret_u, rsem.at[2], rsem.at[3], up)
    back_l.start()
    back_u.start()
    back_l.wait()
    back_u.wait()
    for rows, part in (
        (slice(0, 128), att_b[128:256, :]),
        (slice(128, 256), ret_l[...]),
        (slice(256, 384), ret_u[...]),
        (slice(384, 512), att_b[256:384, :]),
    ):
        att[rows, 512:640] = edge[rows, :] + part[:, 0:128]
        att[rows, 640:1152] = part[:, 128:640]

    for b in range(2):
        result = dot_nt(att[256 * b:256 * b + 256, :], wot[...])
        obuf[:, b] = result.reshape(32, 8, D).astype(BF)

    def send_out(k, carry):
        d = lax.rem(j + k, NSEQ)
        rdma(obuf.at[d], out_ref.at[j], osend, orecv, (s, d)).start()
        return carry

    lax.fori_loop(1, NSEQ, send_out, 0)
    own_out = pltpu.make_async_copy(obuf.at[j], out_ref.at[j], lsem.at[2])
    own_out.start()

    shipped(zsend, 0)

    @pl.when(odd)
    def _():
        shipped(zsend, 1)
        shipped(xsend, 0)

    for i in range(6):
        shipped(ysend, i)
    for i in range(1, 8):
        shipped(xsend, i)
    for i in range(16):
        shipped(ssend, i)
    own_out.wait()
    many = pl.ds(0, NSEQ - 1)
    rdma(hbuf.at[many], xbuf.at[many], tsend, trecv, sib).wait_send()
    rdma(obuf.at[many], out_ref.at[many], osend, orecv, sib).wait_send()
    rdma(obuf.at[many], out_ref.at[many], osend, orecv, sib).wait_recv()


def per_device(video_tokens, modulation, qkv_weight, out_weight):
    vmem = pl.BlockSpec(memory_space=pltpu.VMEM)
    anywhere = pl.BlockSpec(memory_space=pl.ANY)
    projected = pl.pallas_call(
        kernel,
        out_shape=jax.ShapeDtypeStruct((NSEQ, 2, 8, D), BF),
        in_specs=[vmem, vmem, anywhere, anywhere],
        out_specs=anywhere,
        scratch_shapes=[
            pltpu.VMEM((NSEQ, 2, 8, D), BF),
            pltpu.VMEM((NSEQ, 2, 8, D), BF),
            pltpu.VMEM((NSEQ, QROWS, D), BF),
            pltpu.VMEM((NSEQ, OROWS, D), BF),
            pltpu.VMEM((3 * D, D), BF),
            pltpu.VMEM((D, D), BF),
            pltpu.VMEM((512, D), BF),
            pltpu.VMEM((512, D), BF),
            pltpu.VMEM((16, 8, D), BF),
            pltpu.VMEM((16, 8, D), BF),
            pltpu.VMEM((512, WIDE), BF),
            pltpu.VMEM((WIDE, 512), BF),
            pltpu.VMEM((512, WIDE), BF),
            pltpu.VMEM((512, D), BF),
            pltpu.VMEM((512, WIDE), BF),
            pltpu.VMEM((512, 128), BF),
            pltpu.VMEM((128, WIDE), BF),
            pltpu.VMEM((128, WIDE), BF),
            pltpu.VMEM((NSEQ, 2, 8, D), BF),
            pltpu.SemaphoreType.DMA((2, NSEQ)),
            pltpu.SemaphoreType.DMA((2, 2)),
            pltpu.SemaphoreType.DMA((2, 6)),
            pltpu.SemaphoreType.DMA((2, 8)),
            pltpu.SemaphoreType.DMA((2, 16)),
            pltpu.SemaphoreType.DMA((3,)),
            pltpu.SemaphoreType.DMA,
            pltpu.SemaphoreType.DMA,
            pltpu.SemaphoreType.DMA((4,)),
            pltpu.SemaphoreType.DMA((4,)),
            pltpu.SemaphoreType.DMA,
            pltpu.SemaphoreType.DMA,
        ],
        compiler_params=pltpu.CompilerParams(
            collective_id=0, has_side_effects=True, vmem_limit_bytes=60 * 2**20
        ),
    )(
        video_tokens.reshape(512, D),
        modulation.reshape(3, D),
        qkv_weight.T,
        out_weight.T,
    )
    frame_major = projected.reshape(1, 512, D)
    restored = video_tokens.astype(F32) + modulation[:, 2][:, None, :] * frame_major.astype(F32)
    return restored.astype(BF)


def solution(mesh):
    return jax.shard_map(
        per_device,
        mesh=mesh,
        in_specs=(
            P(("slab", "seq"), None, None),
            P(("slab", "seq"), None, None),
            P(None, "seq"),
            P(None, "seq"),
        ),
        out_specs=P(("slab", "seq"), None, None),
        check_vma=False,
    )
```

```python
import functools

import jax
import jax.numpy as jnp
from jax import lax
from jax.experimental import pallas as pl
from jax.experimental.pallas import tpu as pltpu
from jax.sharding import PartitionSpec as P

D = 1152
HEAD = 72
GROUP = 576
WIDE = 640
NSEQ = 32
NSLAB = 16
QROWS = 108
OROWS = 36
MESH = pl.DeviceIdType.MESH
EPS = 1e-06
BF = jnp.bfloat16
F32 = jnp.float32


def dot_nt(a, b):
    return lax.dot_general(a, b, (((1,), (1,)), ((), ())), preferred_element_type=F32)


def kernel(
    tok_ref, mod_ref, qw_ref, ow_ref, out_ref,
    hbuf, xbuf, wq, wo, wt, wot, xa, xb, halo_l, halo_u,
    qs, kts, vs, att, att_b, edge, ret_l, ret_u, obuf,
    wrecv, zsend, ysend, xsend, ssend, lsem, tsend, trecv, hsend, hrecv, osend, orecv,
):
    s = lax.axis_index("slab")
    j = lax.axis_index("seq")
    x = lax.rem(s, 4)
    zh = lax.div(s, 4)
    y = lax.div(j, 8)
    zl = lax.rem(lax.div(j, 2), 4)
    c = lax.rem(j, 2)
    even = lax.rem(x, 2) == 0
    odd = lax.rem(x, 2) == 1
    par = lax.rem(x, 2)

    def zdev(off):
        zz = lax.rem(zh * 4 + zl + off + 16, 16)
        return (lax.div(zz, 4) * 4 + x, y * 8 + lax.rem(zz, 4) * 2 + c)

    def ydev(off):
        return (s, lax.rem(y + off + 4, 4) * 8 + zl * 2 + c)

    def xdev(off):
        return (zh * 4 + lax.rem(x + off + 4, 4), j)

    sib = (s, y * 8 + zl * 2 + (1 - c))
    def rdma(src, dst, ssem, rsem_, dev):
        return pltpu.make_async_remote_copy(
            src_ref=src, dst_ref=dst, send_sem=ssem, recv_sem=rsem_,
            device_id=dev, device_id_type=MESH,
        )

    barrier = pltpu.get_barrier_semaphore()

    def greet(k, carry):
        pl.semaphore_signal(
            barrier, inc=1, device_id=(s, lax.rem(j + k, NSEQ)), device_id_type=MESH
        )
        return carry

    lax.fori_loop(1, NSEQ, greet, 0)
    for dev in (xdev(1), xdev(-1), xdev(2), zdev(1), zdev(-1), zdev(2), zdev(-2)):
        pl.semaphore_signal(barrier, inc=1, device_id=dev, device_id_type=MESH)
    for q in range(4):
        for block in (zh + 1, zh + 3):
            pl.semaphore_signal(
                barrier, inc=1, device_id=(lax.rem(block, 4) * 4 + q, j), device_id_type=MESH
            )
    own_q = pltpu.make_async_copy(qw_ref, wq.at[j], lsem.at[0])
    own_o = pltpu.make_async_copy(ow_ref, wo.at[j], lsem.at[1])
    own_q.start()
    own_o.start()

    shift = mod_ref[0]
    scale = 1.0 + mod_ref[1]

    def norm(i, carry):
        rows = pl.ds(pl.multiple_of(i * 64, 64), 64)
        values = tok_ref[rows, :].astype(F32)
        centered = values - jnp.mean(values, axis=-1, keepdims=True)
        variance = jnp.mean(centered * centered, axis=-1, keepdims=True)
        normed = centered * lax.rsqrt(variance + EPS) * scale + shift
        hbuf[pl.ds(i * 4, 4)] = normed.reshape(4, 2, 8, D).astype(BF)
        return carry

    lax.fori_loop(0, 8, norm, 0)
    own_q.wait()
    own_o.wait()
    pl.semaphore_wait(barrier, NSEQ - 1 + 15)

    def slot(yo, zo):
        return lax.rem(y + yo, 4) * 8 + lax.rem(zl + zo, 4) * 2 + c

    bufs = (wq, wo)

    def ship(t, q, sems, i, dev):
        rdma(bufs[t].at[q], bufs[t].at[q], sems.at[t, i], wrecv.at[t, q], dev).start()

    def shipped(t, sems, i):
        rdma(bufs[t].at[0], bufs[t].at[0], sems.at[t, i], wrecv.at[t, 0], sib).wait_send()

    def landed(t, q):
        rdma(bufs[t].at[q], bufs[t].at[q], zsend.at[t, 0], wrecv.at[t, q], sib).wait_recv()

    za = par * 3
    zb = 1 + par
    oa = (1 - par) * 3
    ob = 2 - par
    plus = ((0, 0), (0, 2), (1, 1), (1, 3))

    def x_ship(t, kind, yo, q):
        ship(t, q, xsend, kind * 4 + yo, xdev(1 if (kind, yo) in plus else -1))

    def stage_z(t):
        @pl.when(even)
        def _():
            ship(t, j, zsend, 0, zdev(-1))
            ship(t, j, ysend, 0, ydev(1))
            ship(t, j, ysend, 1, ydev(-1))

        @pl.when(odd)
        def _():
            ship(t, j, zsend, 1, zdev(-2))
            ship(t, j, zsend, 0, zdev(1))

        ship(t, j, ssend, 0, sib)

    def stage_ab(t):
        @pl.when(odd)
        def _():
            q = slot(0, za)
            landed(t, q)
            ship(t, q, ysend, 0, ydev(1))
            ship(t, q, ysend, 1, ydev(-1))
            x_ship(t, 0, 0, q)
            ship(t, q, ssend, 1, sib)

        q = slot(0, zb)
        landed(t, q)
        ship(t, q, ysend, 2, ydev(1))
        ship(t, q, ysend, 3, ydev(-1))
        x_ship(t, 1, 0, q)
        ship(t, q, ssend, 2, sib)

    near = ((0, 3), (0, 1), (1, 1), (1, 3))
    far = ((0, 2), (1, 2))

    def stage_y(t, which, n):
        for kind, yo in which:
            q = slot(yo, zb if kind else za)
            landed(t, q)
            if (kind, yo) == (0, 3):
                ship(t, q, ysend, 4, ydev(1))
            if (kind, yo) == (1, 1):
                ship(t, q, ysend, 5, ydev(-1))
            x_ship(t, kind, yo, q)
            ship(t, q, ssend, n, sib)
            n += 1

    def stage_x(t):
        @pl.when(even)
        def _():
            q = slot(0, oa)
            landed(t, q)
            ship(t, q, ssend, 1, sib)

        n = 9
        for kind, yo in ((1, 0), (0, 1), (0, 3), (1, 1), (1, 3), (0, 2), (1, 2)):
            q = slot(yo, ob if kind else oa)
            landed(t, q)
            ship(t, q, ssend, n, sib)
            n += 1

    def stage_s(t):
        def other(i, carry):
            landed(t, i * 2 + 1 - c)
            return carry

        lax.fori_loop(0, 16, other, 0)

    last = lax.div(x, 3)
    first = lax.div(3 - x, 3)

    def go_up(pieces, buf, ss, rs):
        for q in range(4):
            dest = (1 - last) * (s + 1) + last * (lax.rem(zh + 1, 4) * 4 + q)
            place = q + last * (4 - q) if q > 0 else 0
            rdma(pieces(q), buf.at[place], ss.at[q], rs.at[place], (dest, j)).start()

    def go_down(pieces, buf, ss, rs):
        for q in range(4):
            dest = (1 - first) * (s - 1) + first * (lax.rem(zh + 3, 4) * 4 + q)
            place = q + first * (4 - q) if q < 3 else 3
            rdma(pieces(q), buf.at[place], ss.at[q], rs.at[place], (dest, j)).start()

    def pass_up(buf, ss, rs):
        @pl.when(x > 0)
        def _():
            rdma(buf.at[4], buf.at[4], ss.at[4], rs.at[4], sib).wait_recv()
            rdma(buf.at[4], buf.at[x], ss.at[4], rs.at[x], (zh * 4, j)).start()

    def pass_down(buf, ss, rs):
        @pl.when(x < 3)
        def _():
            rdma(buf.at[4], buf.at[4], ss.at[4], rs.at[4], sib).wait_recv()
            rdma(buf.at[4], buf.at[x], ss.at[4], rs.at[x], (zh * 4 + 3, j)).start()

    def arrived(buf, ss, rs):
        for q in range(4):
            rdma(buf.at[q], buf.at[q], ss.at[q], rs.at[q], sib).wait_recv()

    def departed(buf, ss, rs, relayed):
        for q in range(4):
            rdma(buf.at[q], buf.at[q], ss.at[q], rs.at[q], sib).wait_send()

        @pl.when(relayed)
        def _():
            rdma(buf.at[4], buf.at[4], ss.at[4], rs.at[4], sib).wait_send()

    stage_z(0)

    def send_tokens(k, carry):
        d = lax.rem(j + k, NSEQ)
        rdma(hbuf.at[d], xbuf.at[j], tsend, trecv, (s, d)).start()
        return carry

    lax.fori_loop(1, NSEQ, send_tokens, 0)
    own_tok = pltpu.make_async_copy(hbuf.at[j], xbuf.at[j], lsem.at[2])
    own_tok.start()

    stage_z(1)
    stage_ab(0)
    stage_y(0, near, 3)
    stage_y(0, far, 7)
    stage_ab(1)

    own_tok.wait()
    rdma(xbuf.at[pl.ds(0, NSEQ - 1)], xbuf.at[pl.ds(0, NSEQ - 1)], tsend, trecv, sib).wait_recv()
    go_up(lambda q: xbuf.at[pl.ds(16 + 4 * q, 4), 0], halo_l, hsend.at[0], hrecv.at[0])
    go_down(lambda q: xbuf.at[pl.ds(4 * q, 4), 1], halo_u, hsend.at[1], hrecv.at[1])

    for b in range(2):
        rows = xbuf[:, b].astype(F32).reshape(256, D).astype(BF)
        xa[256 * b:256 * b + 256, :] = rows
    xb[128:256, :] = xa[0:128, :]
    xb[256:384, :] = xa[384:512, :]

    stage_y(1, near, 3)
    stage_x(0)
    pass_up(halo_l, hsend.at[0], hrecv.at[0])
    pass_down(halo_u, hsend.at[1], hrecv.at[1])
    stage_y(1, far, 7)
    stage_s(0)
    for i in range(16):
        wt[216 * i:216 * i + 216, :] = jnp.concatenate([wq[2 * i], wq[2 * i + 1]], axis=0)

    def project(g, rows_ref):
        base = 1728 * g
        vbase = 2816 if g else 1152
        rows = rows_ref[...]
        qs[...] = dot_nt(rows, wt[base:base + WIDE, :]).astype(BF)
        kts[...] = dot_nt(wt[base + GROUP:base + GROUP + WIDE, :], rows).astype(BF)
        vs[...] = dot_nt(rows, wt[vbase:vbase + WIDE, :]).astype(BF)

    def attend(g, store):
        phase = 64 * g
        row_id = lax.broadcasted_iota(jnp.int32, (256, 256), 0)
        col_id = lax.broadcasted_iota(jnp.int32, (256, 256), 1)
        same = lax.rem(row_id, 8) == lax.rem(col_id, 8)

        def block(b, carry):
            at = pl.ds(pl.multiple_of(b * 256, 256), 256)
            tiles = {}
            for h in range(8):
                lo = HEAD * h
                t0, t1 = lo // 128, (lo + HEAD - 1) // 128
                width = 128 * (t1 - t0 + 1)
                r = lax.broadcasted_iota(jnp.int32, (width, 256), 0) + t0 * 128
                keep = jnp.where((r >= lo) & (r < lo + HEAD), 1.0, 0.0).astype(BF)
                kt = kts[t0 * 128:t0 * 128 + width, at] * keep
                scores = jnp.dot(
                    qs[at, t0 * 128:t0 * 128 + width], kt, preferred_element_type=F32
                ) * (HEAD ** -0.5)
                scores = jnp.where(same, scores, -1e30)
                top = jnp.max(scores, axis=-1, keepdims=True)
                e = jnp.exp(scores - top)
                p = (e * (1.0 / jnp.sum(e, axis=-1, keepdims=True))).astype(BF)
                lo = HEAD * h + phase
                t0, t1 = lo // 128, (lo + HEAD - 1) // 128
                width = 128 * (t1 - t0 + 1)
                r = lax.broadcasted_iota(jnp.int32, (256, width), 1) + t0 * 128
                keep = jnp.where((r >= lo) & (r < lo + HEAD), 1.0, 0.0).astype(BF)
                v = vs[at, t0 * 128:t0 * 128 + width] * keep
                o = jnp.dot(p, v, preferred_element_type=F32)
                for t in range(t0, t1 + 1):
                    piece = o[:, (t - t0) * 128:(t - t0 + 1) * 128]
                    tiles[t] = tiles[t] + piece if t in tiles else piece
                for t in list(tiles):
                    if h == 7 or t < (HEAD * (h + 1) + phase) // 128:
                        store(at, t, tiles.pop(t).astype(BF))
            return carry

        lax.fori_loop(0, 2, block, 0)

    def store_a(at, t, value):
        if t < 4:
            att[at, t * 128:t * 128 + 128] = value
        else:
            edge[at, :] = value

    def store_b(at, t, value):
        att_b[at, t * 128:t * 128 + 128] = value

    project(0, xa)
    attend(0, store_a)

    stage_x(1)
    arrived(halo_l, hsend.at[0], hrecv.at[0])
    arrived(halo_u, hsend.at[1], hrecv.at[1])
    xb[0:128, :] = halo_l[0:4].astype(F32).reshape(128, D).astype(BF)
    xb[384:512, :] = halo_u[0:4].astype(F32).reshape(128, D).astype(BF)
    project(1, xb)
    attend(1, store_b)

    go_down(lambda q: att_b.at[pl.ds(32 * q, 32)], ret_l, hsend.at[2], hrecv.at[2])
    go_up(lambda q: att_b.at[pl.ds(384 + 32 * q, 32)], ret_u, hsend.at[3], hrecv.at[3])

    stage_s(1)
    for i in range(16):
        wot[72 * i:72 * i + 72, :] = jnp.concatenate([wo[2 * i], wo[2 * i + 1]], axis=0)

    def finish(rows, part):
        att[rows, 512:640] = edge[rows, :] + part[:, 0:128]
        att[rows, 640:1152] = part[:, 128:640]
        return dot_nt(att[rows, :], wot[...]).reshape(16, 8, D).astype(BF)

    def send_half(low, high):
        def send_out(k, carry):
            d = lax.rem(j + k, NSEQ)
            b = lax.div(d, 16) * (high - low) + low
            rdma(obuf.at[d, b], out_ref.at[j, b], osend, orecv, (s, d)).start()
            return carry

        lax.fori_loop(1, NSEQ, send_out, 0)

    obuf[0:16, 0] = finish(slice(0, 128), att_b[128:256, :])
    obuf[16:32, 1] = finish(slice(384, 512), att_b[256:384, :])
    send_half(0, 1)
    pass_down(ret_l, hsend.at[2], hrecv.at[2])
    pass_up(ret_u, hsend.at[3], hrecv.at[3])
    arrived(ret_l, hsend.at[2], hrecv.at[2])
    obuf[16:32, 0] = finish(slice(128, 256), ret_l[0:4].reshape(128, WIDE))
    arrived(ret_u, hsend.at[3], hrecv.at[3])
    obuf[0:16, 1] = finish(slice(256, 384), ret_u[0:4].reshape(128, WIDE))
    send_half(1, 0)
    own_out = pltpu.make_async_copy(obuf.at[j], out_ref.at[j], lsem.at[2])
    own_out.start()

    for t in range(2):
        shipped(t, zsend, 0)

        @pl.when(odd)
        def _():
            shipped(t, zsend, 1)
            shipped(t, xsend, 0)

        for i in range(6):
            shipped(t, ysend, i)
        for i in range(1, 8):
            shipped(t, xsend, i)
        for i in range(16):
            shipped(t, ssend, i)
    departed(halo_l, hsend.at[0], hrecv.at[0], x > 0)
    departed(halo_u, hsend.at[1], hrecv.at[1], x < 3)
    departed(ret_l, hsend.at[2], hrecv.at[2], x < 3)
    departed(ret_u, hsend.at[3], hrecv.at[3], x > 0)
    own_out.wait()
    many = pl.ds(0, NSEQ - 1)
    rdma(hbuf.at[many], xbuf.at[many], tsend, trecv, sib).wait_send()
    rdma(obuf.at[many], out_ref.at[many], osend, orecv, sib).wait_send()
    rdma(obuf.at[many], out_ref.at[many], osend, orecv, sib).wait_recv()


def per_device(video_tokens, modulation, qkv_weight, out_weight):
    vmem = pl.BlockSpec(memory_space=pltpu.VMEM)
    anywhere = pl.BlockSpec(memory_space=pl.ANY)
    projected = pl.pallas_call(
        kernel,
        out_shape=jax.ShapeDtypeStruct((NSEQ, 2, 8, D), BF),
        in_specs=[vmem, vmem, anywhere, anywhere],
        out_specs=anywhere,
        scratch_shapes=[
            pltpu.VMEM((NSEQ, 2, 8, D), BF),
            pltpu.VMEM((NSEQ, 2, 8, D), BF),
            pltpu.VMEM((NSEQ, QROWS, D), BF),
            pltpu.VMEM((NSEQ, OROWS, D), BF),
            pltpu.VMEM((3 * D, D), BF),
            pltpu.VMEM((D, D), BF),
            pltpu.VMEM((512, D), BF),
            pltpu.VMEM((512, D), BF),
            pltpu.VMEM((5, 4, 8, D), BF),
            pltpu.VMEM((5, 4, 8, D), BF),
            pltpu.VMEM((512, WIDE), BF),
            pltpu.VMEM((WIDE, 512), BF),
            pltpu.VMEM((512, WIDE), BF),
            pltpu.VMEM((512, D), BF),
            pltpu.VMEM((512, WIDE), BF),
            pltpu.VMEM((512, 128), BF),
            pltpu.VMEM((5, 32, WIDE), BF),
            pltpu.VMEM((5, 32, WIDE), BF),
            pltpu.VMEM((NSEQ, 2, 8, D), BF),
            pltpu.SemaphoreType.DMA((2, NSEQ)),
            pltpu.SemaphoreType.DMA((2, 2)),
            pltpu.SemaphoreType.DMA((2, 6)),
            pltpu.SemaphoreType.DMA((2, 8)),
            pltpu.SemaphoreType.DMA((2, 16)),
            pltpu.SemaphoreType.DMA((3,)),
            pltpu.SemaphoreType.DMA,
            pltpu.SemaphoreType.DMA,
            pltpu.SemaphoreType.DMA((4, 5)),
            pltpu.SemaphoreType.DMA((4, 5)),
            pltpu.SemaphoreType.DMA,
            pltpu.SemaphoreType.DMA,
        ],
        compiler_params=pltpu.CompilerParams(
            collective_id=0, has_side_effects=True, vmem_limit_bytes=60 * 2**20
        ),
    )(
        video_tokens.reshape(512, D),
        modulation.transpose(1, 0, 2),
        qkv_weight.T,
        out_weight.T,
    )
    frame_major = projected.reshape(1, 512, D)
    restored = video_tokens.astype(F32) + modulation[:, 2][:, None, :] * frame_major.astype(F32)
    return restored.astype(BF)


def solution(mesh):
    return jax.shard_map(
        per_device,
        mesh=mesh,
        in_specs=(
            P(("slab", "seq"), None, None),
            P(("slab", "seq"), None, None),
            P(None, "seq"),
            P(None, "seq"),
        ),
        out_specs=P(("slab", "seq"), None, None),
        check_vma=False,
    )
```

```python
import functools

import jax
import jax.numpy as jnp
from jax import lax
from jax.experimental import pallas as pl
from jax.experimental.pallas import tpu as pltpu
from jax.sharding import PartitionSpec as P

D = 1152
HEAD = 72
GROUP = 576
WIDE = 640
NSEQ = 32
NSLAB = 16
QROWS = 108
OROWS = 36
MESH = pl.DeviceIdType.MESH
EPS = 1e-06
BF = jnp.bfloat16
F32 = jnp.float32


def dot_nt(a, b):
    return lax.dot_general(a, b, (((1,), (1,)), ((), ())), preferred_element_type=F32)


def kernel(
    tok_ref, mod_ref, qw_ref, ow_ref, out_ref,
    hbuf, xbuf, wq, wo, wt, wot, xa, xb, halo_l, halo_u,
    qs, kts, vs, att, att_b, edge, ret_l, ret_u, obuf,
    wrecv, zsend, ysend, xsend, ssend, lsem, tsend, trecv, hsend, hrecv, osend, orecv,
):
    s = lax.axis_index("slab")
    j = lax.axis_index("seq")
    x = lax.rem(s, 4)
    zh = lax.div(s, 4)
    y = lax.div(j, 8)
    zl = lax.rem(lax.div(j, 2), 4)
    c = lax.rem(j, 2)
    even = lax.rem(x, 2) == 0
    odd = lax.rem(x, 2) == 1
    par = lax.rem(x, 2)

    def zdev(off):
        zz = lax.rem(zh * 4 + zl + off + 16, 16)
        return (lax.div(zz, 4) * 4 + x, y * 8 + lax.rem(zz, 4) * 2 + c)

    def ydev(off):
        return (s, lax.rem(y + off + 4, 4) * 8 + zl * 2 + c)

    def xdev(off):
        return (zh * 4 + lax.rem(x + off + 4, 4), j)

    sib = (s, y * 8 + zl * 2 + (1 - c))
    def rdma(src, dst, ssem, rsem_, dev):
        return pltpu.make_async_remote_copy(
            src_ref=src, dst_ref=dst, send_sem=ssem, recv_sem=rsem_,
            device_id=dev, device_id_type=MESH,
        )

    barrier = pltpu.get_barrier_semaphore()

    def greet(k, carry):
        pl.semaphore_signal(
            barrier, inc=1, device_id=(s, lax.rem(j + k, NSEQ)), device_id_type=MESH
        )
        return carry

    lax.fori_loop(1, NSEQ, greet, 0)
    for dev in (xdev(1), xdev(-1), xdev(2), zdev(1), zdev(-1), zdev(2), zdev(-2)):
        pl.semaphore_signal(barrier, inc=1, device_id=dev, device_id_type=MESH)
    for q in range(4):
        for block in (zh + 1, zh + 3):
            pl.semaphore_signal(
                barrier, inc=1, device_id=(lax.rem(block, 4) * 4 + q, j), device_id_type=MESH
            )
    own_q = pltpu.make_async_copy(qw_ref, wq.at[j], lsem.at[0])
    own_o = pltpu.make_async_copy(ow_ref, wo.at[j], lsem.at[1])
    own_q.start()
    own_o.start()

    shift = mod_ref[0]
    scale = 1.0 + mod_ref[1]

    def norm(i, carry):
        rows = pl.ds(pl.multiple_of(i * 64, 64), 64)
        values = tok_ref[rows, :].astype(F32)
        centered = values - jnp.mean(values, axis=-1, keepdims=True)
        variance = jnp.mean(centered * centered, axis=-1, keepdims=True)
        normed = centered * lax.rsqrt(variance + EPS) * scale + shift
        hbuf[pl.ds(i * 4, 4)] = normed.reshape(4, 2, 8, D).astype(BF)
        return carry

    lax.fori_loop(0, 8, norm, 0)
    own_q.wait()
    own_o.wait()
    pl.semaphore_wait(barrier, NSEQ - 1 + 15)

    def slot(yo, zo):
        return lax.rem(y + yo, 4) * 8 + lax.rem(zl + zo, 4) * 2 + c

    def part(t, q):
        if t == 2:
            return wo.at[q]
        return wq.at[q, :, pl.ds(0, 640)] if t == 0 else wq.at[q, :, pl.ds(640, 512)]

    def ship(t, q, sems, i, dev):
        rdma(part(t, q), part(t, q), sems.at[t, i], wrecv.at[t, q], dev).start()

    def shipped(t, sems, i):
        rdma(part(t, 0), part(t, 0), sems.at[t, i], wrecv.at[t, 0], sib).wait_send()

    def landed(t, q):
        rdma(part(t, q), part(t, q), zsend.at[t, 0], wrecv.at[t, q], sib).wait_recv()

    za = par * 3
    zb = 1 + par
    oa = (1 - par) * 3
    ob = 2 - par
    plus = ((0, 0), (0, 2), (1, 1), (1, 3))

    def x_ship(t, kind, yo, q):
        ship(t, q, xsend, kind * 4 + yo, xdev(1 if (kind, yo) in plus else -1))

    def stage_z(t):
        @pl.when(even)
        def _():
            ship(t, j, zsend, 0, zdev(-1))
            ship(t, j, ysend, 0, ydev(1))
            ship(t, j, ysend, 1, ydev(-1))

        @pl.when(odd)
        def _():
            ship(t, j, zsend, 1, zdev(-2))
            ship(t, j, zsend, 0, zdev(1))

        ship(t, j, ssend, 0, sib)

    def stage_ab(t):
        @pl.when(odd)
        def _():
            q = slot(0, za)
            landed(t, q)
            ship(t, q, ysend, 0, ydev(1))
            ship(t, q, ysend, 1, ydev(-1))
            x_ship(t, 0, 0, q)
            ship(t, q, ssend, 1, sib)

        q = slot(0, zb)
        landed(t, q)
        ship(t, q, ysend, 2, ydev(1))
        ship(t, q, ysend, 3, ydev(-1))
        x_ship(t, 1, 0, q)
        ship(t, q, ssend, 2, sib)

    near = ((0, 3), (0, 1), (1, 1), (1, 3))
    far = ((0, 2), (1, 2))

    def stage_y(t, which, n):
        for kind, yo in which:
            q = slot(yo, zb if kind else za)
            landed(t, q)
            if (kind, yo) == (0, 3):
                ship(t, q, ysend, 4, ydev(1))
            if (kind, yo) == (1, 1):
                ship(t, q, ysend, 5, ydev(-1))
            x_ship(t, kind, yo, q)
            ship(t, q, ssend, n, sib)
            n += 1

    def stage_x(t):
        @pl.when(even)
        def _():
            q = slot(0, oa)
            landed(t, q)
            ship(t, q, ssend, 1, sib)

        n = 9
        for kind, yo in ((1, 0), (0, 1), (0, 3), (1, 1), (1, 3), (0, 2), (1, 2)):
            q = slot(yo, ob if kind else oa)
            landed(t, q)
            ship(t, q, ssend, n, sib)
            n += 1

    def stage_s(t):
        def other(i, carry):
            landed(t, i * 2 + 1 - c)
            return carry

        lax.fori_loop(0, 16, other, 0)

    last = lax.div(x, 3)
    first = lax.div(3 - x, 3)

    def go_up(pieces, buf, ss, rs):
        for q in range(4):
            far_slab = zh * 4 + q if q < 3 else lax.rem(zh + 1, 4) * 4
            dest = (1 - last) * (s + 1) + last * far_slab
            place = q + last * (4 - q) if q < 3 else 3
            rdma(pieces(q), buf.at[place], ss.at[q], rs.at[place], (dest, j)).start()

    def go_down(pieces, buf, ss, rs):
        for q in range(4):
            far_slab = zh * 4 + q if q > 0 else lax.rem(zh + 3, 4) * 4 + 3
            dest = (1 - first) * (s - 1) + first * far_slab
            place = q + first * (4 - q) if q > 0 else 0
            rdma(pieces(q), buf.at[place], ss.at[q], rs.at[place], (dest, j)).start()

    def pass_up(buf, ss, rs):
        @pl.when(x < 3)
        def _():
            rdma(buf.at[4], buf.at[4], ss.at[4], rs.at[4], sib).wait_recv()
            rdma(buf.at[4], buf.at[x], ss.at[4], rs.at[x], (lax.rem(zh + 1, 4) * 4, j)).start()

    def pass_down(buf, ss, rs):
        @pl.when(x > 0)
        def _():
            rdma(buf.at[4], buf.at[4], ss.at[4], rs.at[4], sib).wait_recv()
            rdma(
                buf.at[4], buf.at[x], ss.at[4], rs.at[x], (lax.rem(zh + 3, 4) * 4 + 3, j)
            ).start()

    def arrived(buf, ss, rs):
        for q in range(4):
            rdma(buf.at[q], buf.at[q], ss.at[q], rs.at[q], sib).wait_recv()

    def departed(buf, ss, rs, relayed):
        for q in range(4):
            rdma(buf.at[q], buf.at[q], ss.at[q], rs.at[q], sib).wait_send()

        @pl.when(relayed)
        def _():
            rdma(buf.at[4], buf.at[4], ss.at[4], rs.at[4], sib).wait_send()

    stage_z(0)
    stage_z(1)

    def send_tokens(k, carry):
        d = lax.rem(j + k, NSEQ)
        rdma(hbuf.at[d], xbuf.at[j], tsend, trecv, (s, d)).start()
        return carry

    lax.fori_loop(1, NSEQ, send_tokens, 0)
    own_tok = pltpu.make_async_copy(hbuf.at[j], xbuf.at[j], lsem.at[2])
    own_tok.start()

    stage_z(2)
    stage_ab(0)
    stage_ab(1)
    stage_y(0, near, 3)
    stage_y(1, near, 3)
    stage_y(0, far, 7)
    stage_y(1, far, 7)
    stage_ab(2)

    own_tok.wait()
    rdma(xbuf.at[pl.ds(0, NSEQ - 1)], xbuf.at[pl.ds(0, NSEQ - 1)], tsend, trecv, sib).wait_recv()
    go_up(lambda q: xbuf.at[pl.ds(16 + 4 * q, 4), 0], halo_l, hsend.at[0], hrecv.at[0])
    go_down(lambda q: xbuf.at[pl.ds(4 * q, 4), 1], halo_u, hsend.at[1], hrecv.at[1])

    for b in range(2):
        rows = xbuf[:, b].astype(F32).reshape(256, D).astype(BF)
        xa[256 * b:256 * b + 256, :] = rows
    xb[128:256, :] = xa[0:128, :]
    xb[256:384, :] = xa[384:512, :]

    pass_up(halo_l, hsend.at[0], hrecv.at[0])
    pass_down(halo_u, hsend.at[1], hrecv.at[1])
    stage_x(0)
    stage_x(1)
    stage_y(2, near, 3)
    stage_y(2, far, 7)
    stage_s(0)
    stage_s(1)
    for i in range(16):
        wt[216 * i:216 * i + 216, :] = jnp.concatenate([wq[2 * i], wq[2 * i + 1]], axis=0)

    def project(g, rows_ref):
        base = 1728 * g
        vbase = 2816 if g else 1152
        rows = rows_ref[...]
        qs[...] = dot_nt(rows, wt[base:base + WIDE, :]).astype(BF)
        kts[...] = dot_nt(wt[base + GROUP:base + GROUP + WIDE, :], rows).astype(BF)
        vs[...] = dot_nt(rows, wt[vbase:vbase + WIDE, :]).astype(BF)

    def attend(g, store):
        phase = 64 * g
        row_id = lax.broadcasted_iota(jnp.int32, (256, 256), 0)
        col_id = lax.broadcasted_iota(jnp.int32, (256, 256), 1)
        same = lax.rem(row_id, 8) == lax.rem(col_id, 8)

        def block(b, carry):
            at = pl.ds(pl.multiple_of(b * 256, 256), 256)
            tiles = {}
            for h in range(8):
                lo = HEAD * h
                t0, t1 = lo // 128, (lo + HEAD - 1) // 128
                width = 128 * (t1 - t0 + 1)
                r = lax.broadcasted_iota(jnp.int32, (width, 256), 0) + t0 * 128
                keep = jnp.where((r >= lo) & (r < lo + HEAD), 1.0, 0.0).astype(BF)
                kt = kts[t0 * 128:t0 * 128 + width, at] * keep
                scores = jnp.dot(
                    qs[at, t0 * 128:t0 * 128 + width], kt, preferred_element_type=F32
                ) * (HEAD ** -0.5)
                scores = jnp.where(same, scores, -1e30)
                top = jnp.max(scores, axis=-1, keepdims=True)
                e = jnp.exp(scores - top)
                p = (e * (1.0 / jnp.sum(e, axis=-1, keepdims=True))).astype(BF)
                lo = HEAD * h + phase
                t0, t1 = lo // 128, (lo + HEAD - 1) // 128
                width = 128 * (t1 - t0 + 1)
                r = lax.broadcasted_iota(jnp.int32, (256, width), 1) + t0 * 128
                keep = jnp.where((r >= lo) & (r < lo + HEAD), 1.0, 0.0).astype(BF)
                v = vs[at, t0 * 128:t0 * 128 + width] * keep
                o = jnp.dot(p, v, preferred_element_type=F32)
                for t in range(t0, t1 + 1):
                    piece = o[:, (t - t0) * 128:(t - t0 + 1) * 128]
                    tiles[t] = tiles[t] + piece if t in tiles else piece
                for t in list(tiles):
                    if h == 7 or t < (HEAD * (h + 1) + phase) // 128:
                        store(at, t, tiles.pop(t).astype(BF))
            return carry

        lax.fori_loop(0, 2, block, 0)

    def store_a(at, t, value):
        if t < 4:
            att[at, t * 128:t * 128 + 128] = value
        else:
            edge[at, :] = value

    def store_b(at, t, value):
        att_b[at, t * 128:t * 128 + 128] = value

    project(0, xa)
    attend(0, store_a)

    stage_x(2)
    arrived(halo_l, hsend.at[0], hrecv.at[0])
    arrived(halo_u, hsend.at[1], hrecv.at[1])
    xb[0:128, :] = halo_l[0:4].astype(F32).reshape(128, D).astype(BF)
    xb[384:512, :] = halo_u[0:4].astype(F32).reshape(128, D).astype(BF)
    project(1, xb)
    attend(1, store_b)

    go_down(lambda q: att_b.at[pl.ds(32 * q, 32)], ret_l, hsend.at[2], hrecv.at[2])
    go_up(lambda q: att_b.at[pl.ds(384 + 32 * q, 32)], ret_u, hsend.at[3], hrecv.at[3])

    stage_s(2)
    for i in range(16):
        wot[72 * i:72 * i + 72, :] = jnp.concatenate([wo[2 * i], wo[2 * i + 1]], axis=0)

    def finish(rows, part):
        att[rows, 512:640] = edge[rows, :] + part[:, 0:128]
        att[rows, 640:1152] = part[:, 128:640]
        return dot_nt(att[rows, :], wot[...]).reshape(16, 8, D).astype(BF)

    def send_half(low, high):
        def send_out(k, carry):
            d = lax.rem(j + k, NSEQ)
            b = lax.div(d, 16) * (high - low) + low
            rdma(obuf.at[d, b], out_ref.at[j, b], osend, orecv, (s, d)).start()
            return carry

        lax.fori_loop(1, NSEQ, send_out, 0)

    obuf[0:16, 0] = finish(slice(0, 128), att_b[128:256, :])
    obuf[16:32, 1] = finish(slice(384, 512), att_b[256:384, :])
    send_half(0, 1)
    pass_down(ret_l, hsend.at[2], hrecv.at[2])
    pass_up(ret_u, hsend.at[3], hrecv.at[3])
    arrived(ret_l, hsend.at[2], hrecv.at[2])
    obuf[16:32, 0] = finish(slice(128, 256), ret_l[0:4].reshape(128, WIDE))
    arrived(ret_u, hsend.at[3], hrecv.at[3])
    obuf[0:16, 1] = finish(slice(256, 384), ret_u[0:4].reshape(128, WIDE))
    send_half(1, 0)
    own_out = pltpu.make_async_copy(obuf.at[j], out_ref.at[j], lsem.at[2])
    own_out.start()

    for t in range(3):
        shipped(t, zsend, 0)

        @pl.when(odd)
        def _():
            shipped(t, zsend, 1)
            shipped(t, xsend, 0)

        for i in range(6):
            shipped(t, ysend, i)
        for i in range(1, 8):
            shipped(t, xsend, i)
        for i in range(16):
            shipped(t, ssend, i)
    departed(halo_l, hsend.at[0], hrecv.at[0], x < 3)
    departed(halo_u, hsend.at[1], hrecv.at[1], x > 0)
    departed(ret_l, hsend.at[2], hrecv.at[2], x > 0)
    departed(ret_u, hsend.at[3], hrecv.at[3], x < 3)
    own_out.wait()
    many = pl.ds(0, NSEQ - 1)
    rdma(hbuf.at[many], xbuf.at[many], tsend, trecv, sib).wait_send()
    rdma(obuf.at[many], out_ref.at[many], osend, orecv, sib).wait_send()
    rdma(obuf.at[many], out_ref.at[many], osend, orecv, sib).wait_recv()


def per_device(video_tokens, modulation, qkv_weight, out_weight):
    vmem = pl.BlockSpec(memory_space=pltpu.VMEM)
    anywhere = pl.BlockSpec(memory_space=pl.ANY)
    projected = pl.pallas_call(
        kernel,
        out_shape=jax.ShapeDtypeStruct((NSEQ, 2, 8, D), BF),
        in_specs=[vmem, vmem, anywhere, anywhere],
        out_specs=anywhere,
        scratch_shapes=[
            pltpu.VMEM((NSEQ, 2, 8, D), BF),
            pltpu.VMEM((NSEQ, 2, 8, D), BF),
            pltpu.VMEM((NSEQ, QROWS, D), BF),
            pltpu.VMEM((NSEQ, OROWS, D), BF),
            pltpu.VMEM((3 * D, D), BF),
            pltpu.VMEM((D, D), BF),
            pltpu.VMEM((512, D), BF),
            pltpu.VMEM((512, D), BF),
            pltpu.VMEM((5, 4, 8, D), BF),
            pltpu.VMEM((5, 4, 8, D), BF),
            pltpu.VMEM((512, WIDE), BF),
            pltpu.VMEM((WIDE, 512), BF),
            pltpu.VMEM((512, WIDE), BF),
            pltpu.VMEM((512, D), BF),
            pltpu.VMEM((512, WIDE), BF),
            pltpu.VMEM((512, 128), BF),
            pltpu.VMEM((5, 32, WIDE), BF),
            pltpu.VMEM((5, 32, WIDE), BF),
            pltpu.VMEM((NSEQ, 2, 8, D), BF),
            pltpu.SemaphoreType.DMA((3, NSEQ)),
            pltpu.SemaphoreType.DMA((3, 2)),
            pltpu.SemaphoreType.DMA((3, 6)),
            pltpu.SemaphoreType.DMA((3, 8)),
            pltpu.SemaphoreType.DMA((3, 16)),
            pltpu.SemaphoreType.DMA((3,)),
            pltpu.SemaphoreType.DMA,
            pltpu.SemaphoreType.DMA,
            pltpu.SemaphoreType.DMA((4, 5)),
            pltpu.SemaphoreType.DMA((4, 5)),
            pltpu.SemaphoreType.DMA,
            pltpu.SemaphoreType.DMA,
        ],
        compiler_params=pltpu.CompilerParams(
            collective_id=0, has_side_effects=True, vmem_limit_bytes=60 * 2**20
        ),
    )(
        video_tokens.reshape(512, D),
        modulation.transpose(1, 0, 2),
        qkv_weight.T,
        out_weight.T,
    )
    frame_major = projected.reshape(1, 512, D)
    restored = video_tokens.astype(F32) + modulation[:, 2][:, None, :] * frame_major.astype(F32)
    return restored.astype(BF)


def solution(mesh):
    return jax.shard_map(
        per_device,
        mesh=mesh,
        in_specs=(
            P(("slab", "seq"), None, None),
            P(("slab", "seq"), None, None),
            P(None, "seq"),
            P(None, "seq"),
        ),
        out_specs=P(("slab", "seq"), None, None),
        check_vma=False,
    )
```

```python
import functools

import jax
import jax.numpy as jnp
from jax import lax
from jax.experimental import pallas as pl
from jax.experimental.pallas import tpu as pltpu
from jax.sharding import PartitionSpec as P

D = 1152
HEAD = 72
GROUP = 576
WIDE = 640
NSEQ = 32
NSLAB = 16
QROWS = 108
OROWS = 36
MESH = pl.DeviceIdType.MESH
EPS = 1e-06
BF = jnp.bfloat16
F32 = jnp.float32


def dot_nt(a, b):
    return lax.dot_general(a, b, (((1,), (1,)), ((), ())), preferred_element_type=F32)


def kernel(
    tok_ref, mod_ref, qw_ref, ow_ref, out_ref,
    hbuf, xbuf, wq, wo, wt, wot, xa, xb, halo_l, halo_u,
    qs, kts, vs, att, att_b, edge, ret_l, ret_u, obuf,
    wrecv, zsend, ysend, xsend, ssend, lsem, tsend, trecv, hsend, hrecv, osend, orecv,
):
    s = lax.axis_index("slab")
    j = lax.axis_index("seq")
    x = lax.rem(s, 4)
    zh = lax.div(s, 4)
    y = lax.div(j, 8)
    zl = lax.rem(lax.div(j, 2), 4)
    c = lax.rem(j, 2)
    even = lax.rem(x, 2) == 0
    odd = lax.rem(x, 2) == 1
    par = lax.rem(x, 2)

    def zdev(off):
        zz = lax.rem(zh * 4 + zl + off + 16, 16)
        return (lax.div(zz, 4) * 4 + x, y * 8 + lax.rem(zz, 4) * 2 + c)

    def ydev(off):
        return (s, lax.rem(y + off + 4, 4) * 8 + zl * 2 + c)

    def xdev(off):
        return (zh * 4 + lax.rem(x + off + 4, 4), j)

    sib = (s, y * 8 + zl * 2 + (1 - c))
    def rdma(src, dst, ssem, rsem_, dev):
        return pltpu.make_async_remote_copy(
            src_ref=src, dst_ref=dst, send_sem=ssem, recv_sem=rsem_,
            device_id=dev, device_id_type=MESH,
        )

    barrier = pltpu.get_barrier_semaphore()

    def greet(k, carry):
        pl.semaphore_signal(
            barrier, inc=1, device_id=(s, lax.rem(j + k, NSEQ)), device_id_type=MESH
        )
        return carry

    lax.fori_loop(1, NSEQ, greet, 0)
    for dev in (xdev(1), xdev(-1), xdev(2), zdev(1), zdev(-1), zdev(2), zdev(-2)):
        pl.semaphore_signal(barrier, inc=1, device_id=dev, device_id_type=MESH)
    for q in range(4):
        for block in (zh + 1, zh + 3):
            pl.semaphore_signal(
                barrier, inc=1, device_id=(lax.rem(block, 4) * 4 + q, j), device_id_type=MESH
            )
    own_q = pltpu.make_async_copy(qw_ref, wq.at[j], lsem.at[0])
    own_o = pltpu.make_async_copy(ow_ref, wo.at[j], lsem.at[1])
    own_q.start()
    own_o.start()

    shift = mod_ref[0]
    scale = 1.0 + mod_ref[1]

    def norm(i, carry):
        rows = pl.ds(pl.multiple_of(i * 64, 64), 64)
        values = tok_ref[rows, :].astype(F32)
        centered = values - jnp.mean(values, axis=-1, keepdims=True)
        variance = jnp.mean(centered * centered, axis=-1, keepdims=True)
        normed = centered * lax.rsqrt(variance + EPS) * scale + shift
        hbuf[pl.ds(i * 4, 4)] = normed.reshape(4, 2, 8, D).astype(BF)
        return carry

    lax.fori_loop(0, 8, norm, 0)
    own_q.wait()
    own_o.wait()
    pl.semaphore_wait(barrier, NSEQ - 1 + 15)

    def slot(yo, zo):
        return lax.rem(y + yo, 4) * 8 + lax.rem(zl + zo, 4) * 2 + c

    def part(t, q):
        if t == 2:
            return wo.at[q]
        return wq.at[q, :, pl.ds(0, 640)] if t == 0 else wq.at[q, :, pl.ds(640, 512)]

    def ship(t, q, sems, i, dev):
        rdma(part(t, q), part(t, q), sems.at[t, i], wrecv.at[t, q], dev).start()

    def shipped(t, sems, i):
        rdma(part(t, 0), part(t, 0), sems.at[t, i], wrecv.at[t, 0], sib).wait_send()

    def landed(t, q):
        rdma(part(t, q), part(t, q), zsend.at[t, 0], wrecv.at[t, q], sib).wait_recv()

    za = par * 3
    zb = 1 + par
    oa = (1 - par) * 3
    ob = 2 - par
    plus = ((0, 0), (0, 2), (1, 1), (1, 3))

    def x_ship(t, kind, yo, q):
        ship(t, q, xsend, kind * 4 + yo, xdev(1 if (kind, yo) in plus else -1))

    def stage_z(t):
        @pl.when(even)
        def _():
            ship(t, j, zsend, 0, zdev(-1))
            ship(t, j, ysend, 0, ydev(1))
            ship(t, j, ysend, 1, ydev(-1))

        @pl.when(odd)
        def _():
            ship(t, j, zsend, 1, zdev(lax.div(zl, 2) * 4 - 2))
            ship(t, j, zsend, 0, zdev(1))

        ship(t, j, ssend, 0, sib)

    def stage_ab(t):
        @pl.when(odd)
        def _():
            q = slot(0, za)
            landed(t, q)
            ship(t, q, ysend, 0, ydev(1))
            ship(t, q, ysend, 1, ydev(-1))
            x_ship(t, 0, 0, q)
            ship(t, q, ssend, 1, sib)

        q = slot(0, zb)
        landed(t, q)
        ship(t, q, ysend, 2, ydev(1))
        ship(t, q, ysend, 3, ydev(-1))
        x_ship(t, 1, 0, q)
        ship(t, q, ssend, 2, sib)

    near = ((0, 3), (0, 1), (1, 1), (1, 3))
    far = ((0, 2), (1, 2))

    def stage_y(t, which, n):
        for kind, yo in which:
            q = slot(yo, zb if kind else za)
            landed(t, q)
            if (kind, yo) == (0, 3):
                ship(t, q, ysend, 4, ydev(1))
            if (kind, yo) == (1, 1):
                ship(t, q, ysend, 5, ydev(-1))
            x_ship(t, kind, yo, q)
            ship(t, q, ssend, n, sib)
            n += 1

    def stage_x(t):
        @pl.when(even)
        def _():
            q = slot(0, oa)
            landed(t, q)
            ship(t, q, ssend, 1, sib)

        n = 9
        for kind, yo in ((1, 0), (0, 1), (0, 3), (1, 1), (1, 3), (0, 2), (1, 2)):
            q = slot(yo, ob if kind else oa)
            landed(t, q)
            ship(t, q, ssend, n, sib)
            n += 1

    def stage_s(t):
        def other(i, carry):
            landed(t, i * 2 + 1 - c)
            return carry

        lax.fori_loop(0, 16, other, 0)

    last = lax.div(x, 3)
    first = lax.div(3 - x, 3)

    def go_up(pieces, buf, ss, rs):
        for q in range(4):
            far_slab = zh * 4 + q if q < 3 else lax.rem(zh + 1, 4) * 4
            dest = (1 - last) * (s + 1) + last * far_slab
            place = q + last * (4 - q) if q < 3 else 3
            rdma(pieces(q), buf.at[place], ss.at[q], rs.at[place], (dest, j)).start()

    def go_down(pieces, buf, ss, rs):
        for q in range(4):
            far_slab = zh * 4 + q if q > 0 else lax.rem(zh + 3, 4) * 4 + 3
            dest = (1 - first) * (s - 1) + first * far_slab
            place = q + first * (4 - q) if q > 0 else 0
            rdma(pieces(q), buf.at[place], ss.at[q], rs.at[place], (dest, j)).start()

    def pass_up(buf, ss, rs):
        @pl.when(x < 3)
        def _():
            rdma(buf.at[4], buf.at[4], ss.at[4], rs.at[4], sib).wait_recv()
            rdma(buf.at[4], buf.at[x], ss.at[4], rs.at[x], (lax.rem(zh + 1, 4) * 4, j)).start()

    def pass_down(buf, ss, rs):
        @pl.when(x > 0)
        def _():
            rdma(buf.at[4], buf.at[4], ss.at[4], rs.at[4], sib).wait_recv()
            rdma(
                buf.at[4], buf.at[x], ss.at[4], rs.at[x], (lax.rem(zh + 3, 4) * 4 + 3, j)
            ).start()

    def arrived(buf, ss, rs):
        for q in range(4):
            rdma(buf.at[q], buf.at[q], ss.at[q], rs.at[q], sib).wait_recv()

    def departed(buf, ss, rs, relayed):
        for q in range(4):
            rdma(buf.at[q], buf.at[q], ss.at[q], rs.at[q], sib).wait_send()

        @pl.when(relayed)
        def _():
            rdma(buf.at[4], buf.at[4], ss.at[4], rs.at[4], sib).wait_send()

    stage_z(0)
    stage_z(1)

    def send_tokens(yo):
        def send(k, carry):
            d = lax.rem(y + yo, 4) * 8 + lax.rem(zl * 2 + c + k, 8)
            rdma(hbuf.at[d], xbuf.at[j], tsend, trecv, (s, d)).start()
            return carry

        lax.fori_loop(0 if yo else 1, 8, send, 0)

    send_tokens(0)
    send_tokens(1)
    send_tokens(3)
    own_tok = pltpu.make_async_copy(hbuf.at[j], xbuf.at[j], lsem.at[2])
    own_tok.start()

    stage_ab(0)
    stage_ab(1)
    send_tokens(2)
    stage_y(0, near, 3)
    stage_y(1, near, 3)
    stage_z(2)
    stage_y(0, far, 7)
    stage_y(1, far, 7)

    own_tok.wait()
    rdma(xbuf.at[pl.ds(0, NSEQ - 1)], xbuf.at[pl.ds(0, NSEQ - 1)], tsend, trecv, sib).wait_recv()
    go_up(lambda q: xbuf.at[pl.ds(16 + 4 * q, 4), 0], halo_l, hsend.at[0], hrecv.at[0])
    go_down(lambda q: xbuf.at[pl.ds(4 * q, 4), 1], halo_u, hsend.at[1], hrecv.at[1])

    for b in range(2):
        rows = xbuf[:, b].astype(F32).reshape(256, D).astype(BF)
        xa[256 * b:256 * b + 256, :] = rows
    xb[128:256, :] = xa[0:128, :]
    xb[256:384, :] = xa[384:512, :]

    stage_ab(2)
    stage_x(0)
    stage_x(1)
    stage_s(0)
    stage_s(1)
    for i in range(16):
        wt[216 * i:216 * i + 216, :] = jnp.concatenate([wq[2 * i], wq[2 * i + 1]], axis=0)
    pass_up(halo_l, hsend.at[0], hrecv.at[0])
    pass_down(halo_u, hsend.at[1], hrecv.at[1])
    stage_y(2, near, 3)

    def project(g, rows_ref):
        base = 1728 * g
        vbase = 2816 if g else 1152
        rows = rows_ref[...]
        qs[...] = dot_nt(rows, wt[base:base + WIDE, :]).astype(BF)
        kts[...] = dot_nt(wt[base + GROUP:base + GROUP + WIDE, :], rows).astype(BF)
        vs[...] = dot_nt(rows, wt[vbase:vbase + WIDE, :]).astype(BF)

    def attend(g, store):
        phase = 64 * g
        row_id = lax.broadcasted_iota(jnp.int32, (256, 256), 0)
        col_id = lax.broadcasted_iota(jnp.int32, (256, 256), 1)
        same = lax.rem(row_id, 8) == lax.rem(col_id, 8)

        def block(b, carry):
            at = pl.ds(pl.multiple_of(b * 256, 256), 256)
            tiles = {}
            for h in range(8):
                lo = HEAD * h
                t0, t1 = lo // 128, (lo + HEAD - 1) // 128
                width = 128 * (t1 - t0 + 1)
                r = lax.broadcasted_iota(jnp.int32, (width, 256), 0) + t0 * 128
                keep = jnp.where((r >= lo) & (r < lo + HEAD), 1.0, 0.0).astype(BF)
                kt = kts[t0 * 128:t0 * 128 + width, at] * keep
                scores = jnp.dot(
                    qs[at, t0 * 128:t0 * 128 + width], kt, preferred_element_type=F32
                ) * (HEAD ** -0.5)
                scores = jnp.where(same, scores, -1e30)
                top = jnp.max(scores, axis=-1, keepdims=True)
                e = jnp.exp(scores - top)
                p = (e * (1.0 / jnp.sum(e, axis=-1, keepdims=True))).astype(BF)
                lo = HEAD * h + phase
                t0, t1 = lo // 128, (lo + HEAD - 1) // 128
                width = 128 * (t1 - t0 + 1)
                r = lax.broadcasted_iota(jnp.int32, (256, width), 1) + t0 * 128
                keep = jnp.where((r >= lo) & (r < lo + HEAD), 1.0, 0.0).astype(BF)
                v = vs[at, t0 * 128:t0 * 128 + width] * keep
                o = jnp.dot(p, v, preferred_element_type=F32)
                for t in range(t0, t1 + 1):
                    piece = o[:, (t - t0) * 128:(t - t0 + 1) * 128]
                    tiles[t] = tiles[t] + piece if t in tiles else piece
                for t in list(tiles):
                    if h == 7 or t < (HEAD * (h + 1) + phase) // 128:
                        store(at, t, tiles.pop(t).astype(BF))
            return carry

        lax.fori_loop(0, 2, block, 0)

    def store_a(at, t, value):
        if t < 4:
            att[at, t * 128:t * 128 + 128] = value
        else:
            edge[at, :] = value

    def store_b(at, t, value):
        att_b[at, t * 128:t * 128 + 128] = value

    project(0, xa)
    stage_y(2, far, 7)
    attend(0, store_a)
    arrived(halo_l, hsend.at[0], hrecv.at[0])
    arrived(halo_u, hsend.at[1], hrecv.at[1])
    xb[0:128, :] = halo_l[0:4].astype(F32).reshape(128, D).astype(BF)
    xb[384:512, :] = halo_u[0:4].astype(F32).reshape(128, D).astype(BF)
    project(1, xb)
    stage_x(2)
    attend(1, store_b)

    go_down(lambda q: att_b.at[pl.ds(32 * q, 32)], ret_l, hsend.at[2], hrecv.at[2])
    go_up(lambda q: att_b.at[pl.ds(384 + 32 * q, 32)], ret_u, hsend.at[3], hrecv.at[3])

    stage_s(2)
    for i in range(16):
        wot[72 * i:72 * i + 72, :] = jnp.concatenate([wo[2 * i], wo[2 * i + 1]], axis=0)

    def finish(rows, part):
        att[rows, 512:640] = edge[rows, :] + part[:, 0:128]
        att[rows, 640:1152] = part[:, 128:640]
        return dot_nt(att[rows, :], wot[...]).reshape(16, 8, D).astype(BF)

    def send_half(low, high):
        def send_out(k, carry):
            d = lax.rem(j + k, NSEQ)
            b = lax.div(d, 16) * (high - low) + low
            rdma(obuf.at[d, b], out_ref.at[j, b], osend, orecv, (s, d)).start()
            return carry

        lax.fori_loop(1, NSEQ, send_out, 0)

    obuf[0:16, 0] = finish(slice(0, 128), att_b[128:256, :])
    obuf[16:32, 1] = finish(slice(384, 512), att_b[256:384, :])
    pass_down(ret_l, hsend.at[2], hrecv.at[2])
    pass_up(ret_u, hsend.at[3], hrecv.at[3])
    send_half(0, 1)
    arrived(ret_l, hsend.at[2], hrecv.at[2])
    obuf[16:32, 0] = finish(slice(128, 256), ret_l[0:4].reshape(128, WIDE))
    arrived(ret_u, hsend.at[3], hrecv.at[3])
    obuf[0:16, 1] = finish(slice(256, 384), ret_u[0:4].reshape(128, WIDE))
    send_half(1, 0)
    own_out = pltpu.make_async_copy(obuf.at[j], out_ref.at[j], lsem.at[2])
    own_out.start()

    for t in range(3):
        shipped(t, zsend, 0)

        @pl.when(odd)
        def _():
            shipped(t, zsend, 1)
            shipped(t, xsend, 0)

        for i in range(6):
            shipped(t, ysend, i)
        for i in range(1, 8):
            shipped(t, xsend, i)
        for i in range(16):
            shipped(t, ssend, i)
    departed(halo_l, hsend.at[0], hrecv.at[0], x < 3)
    departed(halo_u, hsend.at[1], hrecv.at[1], x > 0)
    departed(ret_l, hsend.at[2], hrecv.at[2], x > 0)
    departed(ret_u, hsend.at[3], hrecv.at[3], x < 3)
    own_out.wait()
    many = pl.ds(0, NSEQ - 1)
    rdma(hbuf.at[many], xbuf.at[many], tsend, trecv, sib).wait_send()
    rdma(obuf.at[many], out_ref.at[many], osend, orecv, sib).wait_send()
    rdma(obuf.at[many], out_ref.at[many], osend, orecv, sib).wait_recv()


def per_device(video_tokens, modulation, qkv_weight, out_weight):
    vmem = pl.BlockSpec(memory_space=pltpu.VMEM)
    anywhere = pl.BlockSpec(memory_space=pl.ANY)
    projected = pl.pallas_call(
        kernel,
        out_shape=jax.ShapeDtypeStruct((NSEQ, 2, 8, D), BF),
        in_specs=[vmem, vmem, anywhere, anywhere],
        out_specs=anywhere,
        scratch_shapes=[
            pltpu.VMEM((NSEQ, 2, 8, D), BF),
            pltpu.VMEM((NSEQ, 2, 8, D), BF),
            pltpu.VMEM((NSEQ, QROWS, D), BF),
            pltpu.VMEM((NSEQ, OROWS, D), BF),
            pltpu.VMEM((3 * D, D), BF),
            pltpu.VMEM((D, D), BF),
            pltpu.VMEM((512, D), BF),
            pltpu.VMEM((512, D), BF),
            pltpu.VMEM((5, 4, 8, D), BF),
            pltpu.VMEM((5, 4, 8, D), BF),
            pltpu.VMEM((512, WIDE), BF),
            pltpu.VMEM((WIDE, 512), BF),
            pltpu.VMEM((512, WIDE), BF),
            pltpu.VMEM((512, D), BF),
            pltpu.VMEM((512, WIDE), BF),
            pltpu.VMEM((512, 128), BF),
            pltpu.VMEM((5, 32, WIDE), BF),
            pltpu.VMEM((5, 32, WIDE), BF),
            pltpu.VMEM((NSEQ, 2, 8, D), BF),
            pltpu.SemaphoreType.DMA((3, NSEQ)),
            pltpu.SemaphoreType.DMA((3, 2)),
            pltpu.SemaphoreType.DMA((3, 6)),
            pltpu.SemaphoreType.DMA((3, 8)),
            pltpu.SemaphoreType.DMA((3, 16)),
            pltpu.SemaphoreType.DMA((3,)),
            pltpu.SemaphoreType.DMA,
            pltpu.SemaphoreType.DMA,
            pltpu.SemaphoreType.DMA((4, 5)),
            pltpu.SemaphoreType.DMA((4, 5)),
            pltpu.SemaphoreType.DMA,
            pltpu.SemaphoreType.DMA,
        ],
        compiler_params=pltpu.CompilerParams(
            collective_id=0, has_side_effects=True, vmem_limit_bytes=60 * 2**20
        ),
    )(
        video_tokens.reshape(512, D),
        modulation.transpose(1, 0, 2),
        qkv_weight.T,
        out_weight.T,
    )
    frame_major = projected.reshape(1, 512, D)
    restored = video_tokens.astype(F32) + modulation[:, 2][:, None, :] * frame_major.astype(F32)
    return restored.astype(BF)


def solution(mesh):
    return jax.shard_map(
        per_device,
        mesh=mesh,
        in_specs=(
            P(("slab", "seq"), None, None),
            P(("slab", "seq"), None, None),
            P(None, "seq"),
            P(None, "seq"),
        ),
        out_specs=P(("slab", "seq"), None, None),
        check_vma=False,
    )
```

```python
import functools

import jax
import jax.numpy as jnp
from jax import lax
from jax.experimental import pallas as pl
from jax.experimental.pallas import tpu as pltpu
from jax.sharding import PartitionSpec as P

D = 1152
HEAD = 72
GROUP = 576
WIDE = 640
NSEQ = 32
NSLAB = 16
QROWS = 108
OROWS = 36
MESH = pl.DeviceIdType.MESH
EPS = 1e-06
BF = jnp.bfloat16
F32 = jnp.float32


def dot_nt(a, b):
    return lax.dot_general(a, b, (((1,), (1,)), ((), ())), preferred_element_type=F32)


def kernel(
    tok_ref, mod_ref, qw_ref, ow_ref, out_ref,
    hbuf, xbuf, wq, wo, wt, wot, xa, xb, halo_l, halo_u,
    qs, kts, vs, att, att_b, edge, ret_l, ret_u, obuf,
    wrecv, zsend, ysend, xsend, ssend, lsem, tsend, trecv, hsend, hrecv, osend, orecv,
):
    s = lax.axis_index("slab")
    j = lax.axis_index("seq")
    x = lax.rem(s, 4)
    zh = lax.div(s, 4)
    y = lax.div(j, 8)
    zl = lax.rem(lax.div(j, 2), 4)
    c = lax.rem(j, 2)
    even = lax.rem(x, 2) == 0
    odd = lax.rem(x, 2) == 1
    par = lax.rem(x, 2)

    def zdev(off):
        zz = lax.rem(zh * 4 + zl + off + 16, 16)
        return (lax.div(zz, 4) * 4 + x, y * 8 + lax.rem(zz, 4) * 2 + c)

    def ydev(off):
        return (s, lax.rem(y + off + 4, 4) * 8 + zl * 2 + c)

    def xdev(off):
        return (zh * 4 + lax.rem(x + off + 4, 4), j)

    sib = (s, y * 8 + zl * 2 + (1 - c))
    def rdma(src, dst, ssem, rsem_, dev):
        return pltpu.make_async_remote_copy(
            src_ref=src, dst_ref=dst, send_sem=ssem, recv_sem=rsem_,
            device_id=dev, device_id_type=MESH,
        )

    barrier = pltpu.get_barrier_semaphore()

    def greet(k, carry):
        pl.semaphore_signal(
            barrier, inc=1, device_id=(s, lax.rem(j + k, NSEQ)), device_id_type=MESH
        )
        return carry

    lax.fori_loop(1, NSEQ, greet, 0)
    for dev in (xdev(1), xdev(-1), xdev(2), zdev(1), zdev(-1), zdev(2), zdev(-2)):
        pl.semaphore_signal(barrier, inc=1, device_id=dev, device_id_type=MESH)
    for q in range(4):
        for block in (zh + 1, zh + 3):
            pl.semaphore_signal(
                barrier, inc=1, device_id=(lax.rem(block, 4) * 4 + q, j), device_id_type=MESH
            )
    own_q = pltpu.make_async_copy(qw_ref, wq.at[j], lsem.at[0])
    own_o = pltpu.make_async_copy(ow_ref, wo.at[j], lsem.at[1])
    own_q.start()
    own_o.start()

    shift = mod_ref[0]
    scale = 1.0 + mod_ref[1]

    def norm(i, carry):
        rows = pl.ds(pl.multiple_of(i * 64, 64), 64)
        values = tok_ref[rows, :].astype(F32)
        centered = values - jnp.mean(values, axis=-1, keepdims=True)
        variance = jnp.mean(centered * centered, axis=-1, keepdims=True)
        normed = centered * lax.rsqrt(variance + EPS) * scale + shift
        hbuf[pl.ds(i * 4, 4)] = normed.reshape(4, 2, 8, D).astype(BF)
        return carry

    lax.fori_loop(0, 8, norm, 0)
    own_q.wait()
    own_o.wait()
    pl.semaphore_wait(barrier, NSEQ - 1 + 15)

    def slot(yo, zo):
        return lax.rem(y + yo, 4) * 8 + lax.rem(zl + zo, 4) * 2 + c

    def part(t, q):
        if t == 2:
            return wo.at[q]
        return wq.at[q, :, pl.ds(0, 640)] if t == 0 else wq.at[q, :, pl.ds(640, 512)]

    def ship(t, q, sems, i, dev):
        rdma(part(t, q), part(t, q), sems.at[t, i], wrecv.at[t, q], dev).start()

    def shipped(t, sems, i):
        rdma(part(t, 0), part(t, 0), sems.at[t, i], wrecv.at[t, 0], sib).wait_send()

    def landed(t, q):
        rdma(part(t, q), part(t, q), zsend.at[t, 0], wrecv.at[t, q], sib).wait_recv()

    za = par * 3
    zb = 1 + par
    oa = (1 - par) * 3
    ob = 2 - par
    plus = ((0, 0), (0, 2), (1, 1), (1, 3))

    def x_ship(t, kind, yo, q):
        right = t == 0 or (t == 2 and (kind, yo) in plus)
        ship(t, q, xsend, kind * 4 + yo, xdev(1 if right else -1))

    def stage_z(t):
        @pl.when(even)
        def _():
            ship(t, j, zsend, 0, zdev(-1))
            ship(t, j, ysend, 0, ydev(1))
            ship(t, j, ysend, 1, ydev(-1))

        @pl.when(odd)
        def _():
            ship(t, j, zsend, 1, zdev(lax.div(zl, 2) * 4 - 2))
            ship(t, j, zsend, 0, zdev(1))

        ship(t, j, ssend, 0, sib)

    def stage_ab(t):
        @pl.when(odd)
        def _():
            q = slot(0, za)
            landed(t, q)
            ship(t, q, ysend, 0, ydev(1))
            ship(t, q, ysend, 1, ydev(-1))
            x_ship(t, 0, 0, q)
            ship(t, q, ssend, 1, sib)

        q = slot(0, zb)
        landed(t, q)
        ship(t, q, ysend, 2, ydev(1))
        ship(t, q, ysend, 3, ydev(-1))
        x_ship(t, 1, 0, q)
        ship(t, q, ssend, 2, sib)

    near = ((0, 3), (0, 1), (1, 1), (1, 3))
    far = ((0, 2), (1, 2))

    def stage_y(t, which, n):
        for kind, yo in which:
            q = slot(yo, zb if kind else za)
            landed(t, q)
            if (kind, yo) == (0, 3):
                ship(t, q, ysend, 4, ydev(1))
            if (kind, yo) == (1, 1):
                ship(t, q, ysend, 5, ydev(-1))
            x_ship(t, kind, yo, q)
            ship(t, q, ssend, n, sib)
            n += 1

    def stage_x(t):
        @pl.when(even)
        def _():
            q = slot(0, oa)
            landed(t, q)
            ship(t, q, ssend, 1, sib)

        n = 9
        for kind, yo in ((1, 0), (0, 1), (0, 3), (1, 1), (1, 3), (0, 2), (1, 2)):
            q = slot(yo, ob if kind else oa)
            landed(t, q)
            ship(t, q, ssend, n, sib)
            n += 1

    def stage_s(t):
        def other(i, carry):
            landed(t, i * 2 + 1 - c)
            return carry

        lax.fori_loop(0, 16, other, 0)

    last = lax.div(x, 3)
    first = lax.div(3 - x, 3)

    def go_up(pieces, buf, ss, rs):
        for q in range(4):
            far_slab = zh * 4 + q if q < 3 else lax.rem(zh + 1, 4) * 4
            dest = (1 - last) * (s + 1) + last * far_slab
            place = q + last * (4 - q) if q < 3 else 3
            rdma(pieces(q), buf.at[place], ss.at[q], rs.at[place], (dest, j)).start()

    def go_down(pieces, buf, ss, rs):
        for q in range(4):
            far_slab = zh * 4 + q if q > 0 else lax.rem(zh + 3, 4) * 4 + 3
            dest = (1 - first) * (s - 1) + first * far_slab
            place = q + first * (4 - q) if q > 0 else 0
            rdma(pieces(q), buf.at[place], ss.at[q], rs.at[place], (dest, j)).start()

    def pass_up(buf, ss, rs):
        @pl.when(x < 3)
        def _():
            rdma(buf.at[4], buf.at[4], ss.at[4], rs.at[4], sib).wait_recv()
            rdma(buf.at[4], buf.at[x], ss.at[4], rs.at[x], (lax.rem(zh + 1, 4) * 4, j)).start()

    def pass_down(buf, ss, rs):
        @pl.when(x > 0)
        def _():
            rdma(buf.at[4], buf.at[4], ss.at[4], rs.at[4], sib).wait_recv()
            rdma(
                buf.at[4], buf.at[x], ss.at[4], rs.at[x], (lax.rem(zh + 3, 4) * 4 + 3, j)
            ).start()

    def arrived(buf, ss, rs):
        for q in range(4):
            rdma(buf.at[q], buf.at[q], ss.at[q], rs.at[q], sib).wait_recv()

    def departed(buf, ss, rs, relayed):
        for q in range(4):
            rdma(buf.at[q], buf.at[q], ss.at[q], rs.at[q], sib).wait_send()

        @pl.when(relayed)
        def _():
            rdma(buf.at[4], buf.at[4], ss.at[4], rs.at[4], sib).wait_send()

    stage_z(0)
    stage_z(1)

    def send_tokens(yo):
        def send(k, carry):
            d = lax.rem(y + yo, 4) * 8 + lax.rem(zl * 2 + c + k, 8)
            rdma(hbuf.at[d], xbuf.at[j], tsend, trecv, (s, d)).start()
            return carry

        lax.fori_loop(0 if yo else 1, 8, send, 0)

    send_tokens(0)
    send_tokens(1)
    send_tokens(3)
    own_tok = pltpu.make_async_copy(hbuf.at[j], xbuf.at[j], lsem.at[2])
    own_tok.start()

    stage_ab(0)
    stage_ab(1)
    send_tokens(2)
    stage_y(0, near, 3)
    stage_y(1, near, 3)
    stage_y(0, far, 7)
    stage_y(1, far, 7)
    stage_z(2)

    own_tok.wait()
    rdma(xbuf.at[pl.ds(0, NSEQ - 1)], xbuf.at[pl.ds(0, NSEQ - 1)], tsend, trecv, sib).wait_recv()
    go_up(lambda q: xbuf.at[pl.ds(16 + 4 * q, 4), 0], halo_l, hsend.at[0], hrecv.at[0])
    go_down(lambda q: xbuf.at[pl.ds(4 * q, 4), 1], halo_u, hsend.at[1], hrecv.at[1])

    for b in range(2):
        rows = xbuf[:, b].astype(F32).reshape(256, D).astype(BF)
        xa[256 * b:256 * b + 256, :] = rows
    xb[128:256, :] = xa[0:128, :]
    xb[256:384, :] = xa[384:512, :]

    stage_x(0)
    stage_x(1)
    stage_ab(2)
    stage_s(0)
    stage_s(1)
    for i in range(16):
        wt[216 * i:216 * i + 216, :] = jnp.concatenate([wq[2 * i], wq[2 * i + 1]], axis=0)
    pass_up(halo_l, hsend.at[0], hrecv.at[0])
    pass_down(halo_u, hsend.at[1], hrecv.at[1])
    stage_y(2, near, 3)

    def project(g, rows_ref):
        base = 1728 * g
        vbase = 2816 if g else 1152
        rows = rows_ref[...]
        qs[...] = dot_nt(rows, wt[base:base + WIDE, :]).astype(BF)
        kts[...] = dot_nt(wt[base + GROUP:base + GROUP + WIDE, :], rows).astype(BF)
        vs[...] = dot_nt(rows, wt[vbase:vbase + WIDE, :]).astype(BF)

    def attend(g, store):
        phase = 64 * g
        row_id = lax.broadcasted_iota(jnp.int32, (256, 256), 0)
        col_id = lax.broadcasted_iota(jnp.int32, (256, 256), 1)
        same = lax.rem(row_id, 8) == lax.rem(col_id, 8)

        def block(b, carry):
            at = pl.ds(pl.multiple_of(b * 256, 256), 256)
            tiles = {}
            for h in range(8):
                lo = HEAD * h
                t0, t1 = lo // 128, (lo + HEAD - 1) // 128
                width = 128 * (t1 - t0 + 1)
                r = lax.broadcasted_iota(jnp.int32, (width, 256), 0) + t0 * 128
                keep = jnp.where((r >= lo) & (r < lo + HEAD), 1.0, 0.0).astype(BF)
                kt = kts[t0 * 128:t0 * 128 + width, at] * keep
                scores = jnp.dot(
                    qs[at, t0 * 128:t0 * 128 + width], kt, preferred_element_type=F32
                ) * (HEAD ** -0.5)
                scores = jnp.where(same, scores, -1e30)
                top = jnp.max(scores, axis=-1, keepdims=True)
                e = jnp.exp(scores - top)
                p = (e * (1.0 / jnp.sum(e, axis=-1, keepdims=True))).astype(BF)
                lo = HEAD * h + phase
                t0, t1 = lo // 128, (lo + HEAD - 1) // 128
                width = 128 * (t1 - t0 + 1)
                r = lax.broadcasted_iota(jnp.int32, (256, width), 1) + t0 * 128
                keep = jnp.where((r >= lo) & (r < lo + HEAD), 1.0, 0.0).astype(BF)
                v = vs[at, t0 * 128:t0 * 128 + width] * keep
                o = jnp.dot(p, v, preferred_element_type=F32)
                for t in range(t0, t1 + 1):
                    piece = o[:, (t - t0) * 128:(t - t0 + 1) * 128]
                    tiles[t] = tiles[t] + piece if t in tiles else piece
                for t in list(tiles):
                    if h == 7 or t < (HEAD * (h + 1) + phase) // 128:
                        store(at, t, tiles.pop(t).astype(BF))
            return carry

        lax.fori_loop(0, 2, block, 0)

    def store_a(at, t, value):
        if t < 4:
            att[at, t * 128:t * 128 + 128] = value
        else:
            edge[at, :] = value

    def store_b(at, t, value):
        att_b[at, t * 128:t * 128 + 128] = value

    project(0, xa)
    attend(0, store_a)
    stage_y(2, far, 7)
    arrived(halo_l, hsend.at[0], hrecv.at[0])
    arrived(halo_u, hsend.at[1], hrecv.at[1])
    xb[0:128, :] = halo_l[0:4].astype(F32).reshape(128, D).astype(BF)
    xb[384:512, :] = halo_u[0:4].astype(F32).reshape(128, D).astype(BF)
    project(1, xb)
    stage_x(2)
    attend(1, store_b)

    go_down(lambda q: att_b.at[pl.ds(32 * q, 32)], ret_l, hsend.at[2], hrecv.at[2])
    go_up(lambda q: att_b.at[pl.ds(384 + 32 * q, 32)], ret_u, hsend.at[3], hrecv.at[3])

    stage_s(2)
    for i in range(16):
        wot[72 * i:72 * i + 72, :] = jnp.concatenate([wo[2 * i], wo[2 * i + 1]], axis=0)

    def finish(rows, part):
        att[rows, 512:640] = edge[rows, :] + part[:, 0:128]
        att[rows, 640:1152] = part[:, 128:640]
        return dot_nt(att[rows, :], wot[...]).reshape(16, 8, D).astype(BF)

    def send_half(low, high, steps):
        for yo in steps:
            def send_out(k, carry, yo=yo):
                d = lax.rem(y + yo, 4) * 8 + lax.rem(zl * 2 + c + k, 8)
                b = lax.div(d, 16) * (high - low) + low
                rdma(obuf.at[d, b], out_ref.at[j, b], osend, orecv, (s, d)).start()
                return carry

            lax.fori_loop(0 if yo else 1, 8, send_out, 0)

    obuf[0:16, 0] = finish(slice(0, 128), att_b[128:256, :])
    obuf[16:32, 1] = finish(slice(384, 512), att_b[256:384, :])
    send_half(0, 1, (0,))
    pass_down(ret_l, hsend.at[2], hrecv.at[2])
    pass_up(ret_u, hsend.at[3], hrecv.at[3])
    send_half(0, 1, (2, 1, 3))
    arrived(ret_l, hsend.at[2], hrecv.at[2])
    obuf[16:32, 0] = finish(slice(128, 256), ret_l[0:4].reshape(128, WIDE))
    arrived(ret_u, hsend.at[3], hrecv.at[3])
    obuf[0:16, 1] = finish(slice(256, 384), ret_u[0:4].reshape(128, WIDE))
    send_half(1, 0, (2, 1, 3, 0))
    own_out = pltpu.make_async_copy(obuf.at[j], out_ref.at[j], lsem.at[2])
    own_out.start()

    for t in range(3):
        shipped(t, zsend, 0)

        @pl.when(odd)
        def _():
            shipped(t, zsend, 1)
            shipped(t, xsend, 0)

        for i in range(6):
            shipped(t, ysend, i)
        for i in range(1, 8):
            shipped(t, xsend, i)
        for i in range(16):
            shipped(t, ssend, i)
    departed(halo_l, hsend.at[0], hrecv.at[0], x < 3)
    departed(halo_u, hsend.at[1], hrecv.at[1], x > 0)
    departed(ret_l, hsend.at[2], hrecv.at[2], x > 0)
    departed(ret_u, hsend.at[3], hrecv.at[3], x < 3)
    own_out.wait()
    many = pl.ds(0, NSEQ - 1)
    rdma(hbuf.at[many], xbuf.at[many], tsend, trecv, sib).wait_send()
    rdma(obuf.at[many], out_ref.at[many], osend, orecv, sib).wait_send()
    rdma(obuf.at[many], out_ref.at[many], osend, orecv, sib).wait_recv()


def per_device(video_tokens, modulation, qkv_weight, out_weight):
    vmem = pl.BlockSpec(memory_space=pltpu.VMEM)
    anywhere = pl.BlockSpec(memory_space=pl.ANY)
    projected = pl.pallas_call(
        kernel,
        out_shape=jax.ShapeDtypeStruct((NSEQ, 2, 8, D), BF),
        in_specs=[vmem, vmem, anywhere, anywhere],
        out_specs=anywhere,
        scratch_shapes=[
            pltpu.VMEM((NSEQ, 2, 8, D), BF),
            pltpu.VMEM((NSEQ, 2, 8, D), BF),
            pltpu.VMEM((NSEQ, QROWS, D), BF),
            pltpu.VMEM((NSEQ, OROWS, D), BF),
            pltpu.VMEM((3 * D, D), BF),
            pltpu.VMEM((D, D), BF),
            pltpu.VMEM((512, D), BF),
            pltpu.VMEM((512, D), BF),
            pltpu.VMEM((5, 4, 8, D), BF),
            pltpu.VMEM((5, 4, 8, D), BF),
            pltpu.VMEM((512, WIDE), BF),
            pltpu.VMEM((WIDE, 512), BF),
            pltpu.VMEM((512, WIDE), BF),
            pltpu.VMEM((512, D), BF),
            pltpu.VMEM((512, WIDE), BF),
            pltpu.VMEM((512, 128), BF),
            pltpu.VMEM((5, 32, WIDE), BF),
            pltpu.VMEM((5, 32, WIDE), BF),
            pltpu.VMEM((NSEQ, 2, 8, D), BF),
            pltpu.SemaphoreType.DMA((3, NSEQ)),
            pltpu.SemaphoreType.DMA((3, 2)),
            pltpu.SemaphoreType.DMA((3, 6)),
            pltpu.SemaphoreType.DMA((3, 8)),
            pltpu.SemaphoreType.DMA((3, 16)),
            pltpu.SemaphoreType.DMA((3,)),
            pltpu.SemaphoreType.DMA,
            pltpu.SemaphoreType.DMA,
            pltpu.SemaphoreType.DMA((4, 5)),
            pltpu.SemaphoreType.DMA((4, 5)),
            pltpu.SemaphoreType.DMA,
            pltpu.SemaphoreType.DMA,
        ],
        compiler_params=pltpu.CompilerParams(
            collective_id=0, has_side_effects=True, vmem_limit_bytes=60 * 2**20
        ),
    )(
        video_tokens.reshape(512, D),
        modulation.transpose(1, 0, 2),
        qkv_weight.T,
        out_weight.T,
    )
    frame_major = projected.reshape(1, 512, D)
    restored = video_tokens.astype(F32) + modulation[:, 2][:, None, :] * frame_major.astype(F32)
    return restored.astype(BF)


def solution(mesh):
    return jax.shard_map(
        per_device,
        mesh=mesh,
        in_specs=(
            P(("slab", "seq"), None, None),
            P(("slab", "seq"), None, None),
            P(None, "seq"),
            P(None, "seq"),
        ),
        out_specs=P(("slab", "seq"), None, None),
        check_vma=False,
    )
```

```python
import functools

import jax
import jax.numpy as jnp
from jax import lax
from jax.experimental import pallas as pl
from jax.experimental.pallas import tpu as pltpu
from jax.sharding import PartitionSpec as P

D = 1152
HEAD = 72
GROUP = 576
WIDE = 640
NSEQ = 32
NSLAB = 16
QROWS = 108
OROWS = 36
MESH = pl.DeviceIdType.MESH
EPS = 1e-06
BF = jnp.bfloat16
F32 = jnp.float32


def dot_nt(a, b):
    return lax.dot_general(a, b, (((1,), (1,)), ((), ())), preferred_element_type=F32)


def kernel(
    tok_ref, mod_ref, qw_ref, ow_ref, out_ref,
    hbuf, xbuf, wq, wo, wt, wot, xa, xb, halo_l, halo_u,
    qs, kts, vs, att, att_b, edge, ret_l, ret_u, obuf,
    wrecv, zsend, ysend, xsend, ssend, lsem, tsend, trecv, hsend, hrecv, osend, orecv,
):
    s = lax.axis_index("slab")
    j = lax.axis_index("seq")
    x = lax.rem(s, 4)
    zh = lax.div(s, 4)
    y = lax.div(j, 8)
    zl = lax.rem(lax.div(j, 2), 4)
    c = lax.rem(j, 2)
    even = lax.rem(x, 2) == 0
    odd = lax.rem(x, 2) == 1
    par = lax.rem(x, 2)

    def zdev(off):
        zz = lax.rem(zh * 4 + zl + off + 16, 16)
        return (lax.div(zz, 4) * 4 + x, y * 8 + lax.rem(zz, 4) * 2 + c)

    def ydev(off):
        return (s, lax.rem(y + off + 4, 4) * 8 + zl * 2 + c)

    def xdev(off):
        return (zh * 4 + lax.rem(x + off + 4, 4), j)

    sib = (s, y * 8 + zl * 2 + (1 - c))
    def rdma(src, dst, ssem, rsem_, dev):
        return pltpu.make_async_remote_copy(
            src_ref=src, dst_ref=dst, send_sem=ssem, recv_sem=rsem_,
            device_id=dev, device_id_type=MESH,
        )

    barrier = pltpu.get_barrier_semaphore()

    def greet(k, carry):
        pl.semaphore_signal(
            barrier, inc=1, device_id=(s, lax.rem(j + k, NSEQ)), device_id_type=MESH
        )
        return carry

    lax.fori_loop(1, NSEQ, greet, 0)
    for dev in (xdev(1), xdev(-1), xdev(2), zdev(1), zdev(-1), zdev(2), zdev(-2)):
        pl.semaphore_signal(barrier, inc=1, device_id=dev, device_id_type=MESH)
    for q in range(4):
        for block in (zh + 1, zh + 3):
            pl.semaphore_signal(
                barrier, inc=1, device_id=(lax.rem(block, 4) * 4 + q, j), device_id_type=MESH
            )
    own_q = pltpu.make_async_copy(qw_ref, wq.at[j], lsem.at[0])
    own_o = pltpu.make_async_copy(ow_ref, wo.at[j], lsem.at[1])
    own_q.start()
    own_o.start()

    shift = mod_ref[0]
    scale = 1.0 + mod_ref[1]

    def norm(i, carry):
        rows = pl.ds(pl.multiple_of(i * 64, 64), 64)
        values = tok_ref[rows, :].astype(F32)
        centered = values - jnp.mean(values, axis=-1, keepdims=True)
        variance = jnp.mean(centered * centered, axis=-1, keepdims=True)
        normed = centered * lax.rsqrt(variance + EPS) * scale + shift
        hbuf[pl.ds(i * 4, 4)] = normed.reshape(4, 2, 8, D).astype(BF)
        return carry

    lax.fori_loop(0, 8, norm, 0)
    own_q.wait()
    own_o.wait()
    pl.semaphore_wait(barrier, NSEQ - 1 + 15)

    def slot(yo, zo):
        return lax.rem(y + yo, 4) * 8 + lax.rem(zl + zo, 4) * 2 + c

    def part(t, q):
        if t == 2:
            return wo.at[q]
        return wq.at[q, :, pl.ds(0, 640)] if t == 0 else wq.at[q, :, pl.ds(640, 512)]

    def ship(t, q, sems, i, dev):
        rdma(part(t, q), part(t, q), sems.at[t, i], wrecv.at[t, q], dev).start()

    def shipped(t, sems, i):
        rdma(part(t, 0), part(t, 0), sems.at[t, i], wrecv.at[t, 0], sib).wait_send()

    def landed(t, q):
        rdma(part(t, q), part(t, q), zsend.at[t, 0], wrecv.at[t, q], sib).wait_recv()

    za = par * 3
    zb = 1 + par
    oa = (1 - par) * 3
    ob = 2 - par
    plus = ((0, 0), (0, 2), (1, 1), (1, 3))

    def x_ship(t, kind, yo, q):
        right = t == 0 or (t == 2 and (kind, yo) in plus)
        ship(t, q, xsend, kind * 4 + yo, xdev(1 if right else -1))

    def own_y(t):
        ship(t, j, ysend, 0, ydev(1))
        ship(t, j, ysend, 1, ydev(-1))

    def stage_z(t):
        @pl.when(even)
        def _():
            ship(t, j, zsend, 0, zdev(-1))
            if t < 2:
                own_y(t)

        @pl.when(odd)
        def _():
            ship(t, j, zsend, 1, zdev(lax.div(zl, 2) * 4 - 2))
            ship(t, j, zsend, 0, zdev(1))

        ship(t, j, ssend, 0, sib)

    def stage_ab(t):
        @pl.when(odd)
        def _():
            q = slot(0, za)
            landed(t, q)
            ship(t, q, ysend, 0, ydev(1))
            ship(t, q, ysend, 1, ydev(-1))
            x_ship(t, 0, 0, q)
            ship(t, q, ssend, 1, sib)

        q = slot(0, zb)
        landed(t, q)
        ship(t, q, ysend, 2, ydev(1))
        ship(t, q, ysend, 3, ydev(-1))
        x_ship(t, 1, 0, q)
        ship(t, q, ssend, 2, sib)

    near = ((0, 3), (0, 1), (1, 1), (1, 3))
    far = ((0, 2), (1, 2))

    def stage_y(t, which, n):
        for kind, yo in which:
            q = slot(yo, zb if kind else za)
            landed(t, q)
            if (kind, yo) == (0, 3):
                ship(t, q, ysend, 4, ydev(1))
            if (kind, yo) == (1, 1):
                ship(t, q, ysend, 5, ydev(-1))
            x_ship(t, kind, yo, q)
            ship(t, q, ssend, n, sib)
            n += 1

    def stage_x(t):
        @pl.when(even)
        def _():
            q = slot(0, oa)
            landed(t, q)
            ship(t, q, ssend, 1, sib)

        n = 9
        for kind, yo in ((1, 0), (0, 1), (0, 3), (1, 1), (1, 3), (0, 2), (1, 2)):
            q = slot(yo, ob if kind else oa)
            landed(t, q)
            ship(t, q, ssend, n, sib)
            n += 1

    def stage_s(t):
        def other(i, carry):
            landed(t, i * 2 + 1 - c)
            return carry

        lax.fori_loop(0, 16, other, 0)

    last = lax.div(x, 3)
    first = lax.div(3 - x, 3)

    def go_up(pieces, buf, ss, rs):
        for q in range(4):
            far_slab = zh * 4 + q if q < 3 else lax.rem(zh + 1, 4) * 4
            dest = (1 - last) * (s + 1) + last * far_slab
            place = q + last * (4 - q) if q < 3 else 3
            rdma(pieces(q), buf.at[place], ss.at[q], rs.at[place], (dest, j)).start()

    def go_down(pieces, buf, ss, rs):
        for q in range(4):
            far_slab = zh * 4 + q if q > 0 else lax.rem(zh + 3, 4) * 4 + 3
            dest = (1 - first) * (s - 1) + first * far_slab
            place = q + first * (4 - q) if q > 0 else 0
            rdma(pieces(q), buf.at[place], ss.at[q], rs.at[place], (dest, j)).start()

    def pass_up(buf, ss, rs):
        @pl.when(x < 3)
        def _():
            rdma(buf.at[4], buf.at[4], ss.at[4], rs.at[4], sib).wait_recv()
            rdma(buf.at[4], buf.at[x], ss.at[4], rs.at[x], (lax.rem(zh + 1, 4) * 4, j)).start()

    def pass_down(buf, ss, rs):
        @pl.when(x > 0)
        def _():
            rdma(buf.at[4], buf.at[4], ss.at[4], rs.at[4], sib).wait_recv()
            rdma(
                buf.at[4], buf.at[x], ss.at[4], rs.at[x], (lax.rem(zh + 3, 4) * 4 + 3, j)
            ).start()

    def arrived(buf, ss, rs):
        for q in range(4):
            rdma(buf.at[q], buf.at[q], ss.at[q], rs.at[q], sib).wait_recv()

    def departed(buf, ss, rs, relayed):
        for q in range(4):
            rdma(buf.at[q], buf.at[q], ss.at[q], rs.at[q], sib).wait_send()

        @pl.when(relayed)
        def _():
            rdma(buf.at[4], buf.at[4], ss.at[4], rs.at[4], sib).wait_send()

    stage_z(0)
    stage_z(1)

    def send_tokens(yo):
        def send(k, carry):
            d = lax.rem(y + yo, 4) * 8 + lax.rem(zl * 2 + c + k, 8)
            rdma(hbuf.at[d], xbuf.at[j], tsend, trecv, (s, d)).start()
            return carry

        lax.fori_loop(0 if yo else 1, 8, send, 0)

    send_tokens(0)
    send_tokens(1)
    send_tokens(3)
    own_tok = pltpu.make_async_copy(hbuf.at[j], xbuf.at[j], lsem.at[2])
    own_tok.start()

    stage_ab(0)
    stage_ab(1)
    send_tokens(2)
    stage_y(0, near, 3)
    stage_y(1, near, 3)
    stage_z(2)
    stage_y(0, far, 7)
    stage_y(1, far, 7)

    own_tok.wait()
    rdma(xbuf.at[pl.ds(0, NSEQ - 1)], xbuf.at[pl.ds(0, NSEQ - 1)], tsend, trecv, sib).wait_recv()
    go_up(lambda q: xbuf.at[pl.ds(16 + 4 * q, 4), 0], halo_l, hsend.at[0], hrecv.at[0])
    go_down(lambda q: xbuf.at[pl.ds(4 * q, 4), 1], halo_u, hsend.at[1], hrecv.at[1])

    for b in range(2):
        rows = xbuf[:, b].astype(F32).reshape(256, D).astype(BF)
        xa[256 * b:256 * b + 256, :] = rows
    xb[128:256, :] = xa[0:128, :]
    xb[256:384, :] = xa[384:512, :]


    @pl.when(even)
    def _():
        own_y(2)

    stage_ab(2)
    stage_x(0)
    stage_x(1)
    pass_up(halo_l, hsend.at[0], hrecv.at[0])
    pass_down(halo_u, hsend.at[1], hrecv.at[1])
    stage_s(0)
    stage_s(1)
    for i in range(16):
        wt[216 * i:216 * i + 216, :] = jnp.concatenate([wq[2 * i], wq[2 * i + 1]], axis=0)
    stage_y(2, near, 3)

    def project(g, rows_ref):
        base = 1728 * g
        vbase = 2816 if g else 1152
        rows = rows_ref[...]
        qs[...] = dot_nt(rows, wt[base:base + WIDE, :]).astype(BF)
        kts[...] = dot_nt(wt[base + GROUP:base + GROUP + WIDE, :], rows).astype(BF)
        vs[...] = dot_nt(rows, wt[vbase:vbase + WIDE, :]).astype(BF)

    def attend(g, store):
        phase = 64 * g
        row_id = lax.broadcasted_iota(jnp.int32, (256, 256), 0)
        col_id = lax.broadcasted_iota(jnp.int32, (256, 256), 1)
        same = lax.rem(row_id, 8) == lax.rem(col_id, 8)

        def block(b, carry):
            at = pl.ds(pl.multiple_of(b * 256, 256), 256)
            tiles = {}
            for h in range(8):
                lo = HEAD * h
                t0, t1 = lo // 128, (lo + HEAD - 1) // 128
                width = 128 * (t1 - t0 + 1)
                r = lax.broadcasted_iota(jnp.int32, (width, 256), 0) + t0 * 128
                keep = jnp.where((r >= lo) & (r < lo + HEAD), 1.0, 0.0).astype(BF)
                kt = kts[t0 * 128:t0 * 128 + width, at] * keep
                scores = jnp.dot(
                    qs[at, t0 * 128:t0 * 128 + width], kt, preferred_element_type=F32
                ) * (HEAD ** -0.5)
                scores = jnp.where(same, scores, -1e30)
                top = jnp.max(scores, axis=-1, keepdims=True)
                e = jnp.exp(scores - top)
                p = (e * (1.0 / jnp.sum(e, axis=-1, keepdims=True))).astype(BF)
                lo = HEAD * h + phase
                t0, t1 = lo // 128, (lo + HEAD - 1) // 128
                width = 128 * (t1 - t0 + 1)
                r = lax.broadcasted_iota(jnp.int32, (256, width), 1) + t0 * 128
                keep = jnp.where((r >= lo) & (r < lo + HEAD), 1.0, 0.0).astype(BF)
                v = vs[at, t0 * 128:t0 * 128 + width] * keep
                o = jnp.dot(p, v, preferred_element_type=F32)
                for t in range(t0, t1 + 1):
                    piece = o[:, (t - t0) * 128:(t - t0 + 1) * 128]
                    tiles[t] = tiles[t] + piece if t in tiles else piece
                for t in list(tiles):
                    if h == 7 or t < (HEAD * (h + 1) + phase) // 128:
                        store(at, t, tiles.pop(t).astype(BF))
            return carry

        lax.fori_loop(0, 2, block, 0)

    def store_a(at, t, value):
        if t < 4:
            att[at, t * 128:t * 128 + 128] = value
        else:
            edge[at, :] = value

    def store_b(at, t, value):
        att_b[at, t * 128:t * 128 + 128] = value

    project(0, xa)
    attend(0, store_a)
    stage_y(2, far, 7)
    arrived(halo_l, hsend.at[0], hrecv.at[0])
    arrived(halo_u, hsend.at[1], hrecv.at[1])
    xb[0:128, :] = halo_l[0:4].astype(F32).reshape(128, D).astype(BF)
    xb[384:512, :] = halo_u[0:4].astype(F32).reshape(128, D).astype(BF)
    project(1, xb)
    stage_x(2)
    attend(1, store_b)

    go_down(lambda q: att_b.at[pl.ds(32 * q, 32)], ret_l, hsend.at[2], hrecv.at[2])
    go_up(lambda q: att_b.at[pl.ds(384 + 32 * q, 32)], ret_u, hsend.at[3], hrecv.at[3])

    stage_s(2)
    for i in range(16):
        wot[72 * i:72 * i + 72, :] = jnp.concatenate([wo[2 * i], wo[2 * i + 1]], axis=0)

    def finish(rows, part):
        att[rows, 512:640] = edge[rows, :] + part[:, 0:128]
        att[rows, 640:1152] = part[:, 128:640]
        return dot_nt(att[rows, :], wot[...]).reshape(16, 8, D).astype(BF)

    def send_half(low, high, steps):
        for yo in steps:
            def send_out(k, carry, yo=yo):
                d = lax.rem(y + yo, 4) * 8 + lax.rem(zl * 2 + c + k, 8)
                b = lax.div(d, 16) * (high - low) + low
                rdma(obuf.at[d, b], out_ref.at[j, b], osend, orecv, (s, d)).start()
                return carry

            lax.fori_loop(0 if yo else 1, 8, send_out, 0)

    obuf[0:16, 0] = finish(slice(0, 128), att_b[128:256, :])
    obuf[16:32, 1] = finish(slice(384, 512), att_b[256:384, :])
    send_half(0, 1, (0,))
    pass_down(ret_l, hsend.at[2], hrecv.at[2])
    pass_up(ret_u, hsend.at[3], hrecv.at[3])
    send_half(0, 1, (2, 1, 3))
    arrived(ret_l, hsend.at[2], hrecv.at[2])
    obuf[16:32, 0] = finish(slice(128, 256), ret_l[0:4].reshape(128, WIDE))
    arrived(ret_u, hsend.at[3], hrecv.at[3])
    obuf[0:16, 1] = finish(slice(256, 384), ret_u[0:4].reshape(128, WIDE))
    send_half(1, 0, (2, 1, 3, 0))
    own_out = pltpu.make_async_copy(obuf.at[j], out_ref.at[j], lsem.at[2])
    own_out.start()

    for t in range(3):
        shipped(t, zsend, 0)

        @pl.when(odd)
        def _():
            shipped(t, zsend, 1)
            shipped(t, xsend, 0)

        for i in range(6):
            shipped(t, ysend, i)
        for i in range(1, 8):
            shipped(t, xsend, i)
        for i in range(16):
            shipped(t, ssend, i)
    departed(halo_l, hsend.at[0], hrecv.at[0], x < 3)
    departed(halo_u, hsend.at[1], hrecv.at[1], x > 0)
    departed(ret_l, hsend.at[2], hrecv.at[2], x > 0)
    departed(ret_u, hsend.at[3], hrecv.at[3], x < 3)
    own_out.wait()
    many = pl.ds(0, NSEQ - 1)
    rdma(hbuf.at[many], xbuf.at[many], tsend, trecv, sib).wait_send()
    rdma(obuf.at[many], out_ref.at[many], osend, orecv, sib).wait_send()
    rdma(obuf.at[many], out_ref.at[many], osend, orecv, sib).wait_recv()


def per_device(video_tokens, modulation, qkv_weight, out_weight):
    vmem = pl.BlockSpec(memory_space=pltpu.VMEM)
    anywhere = pl.BlockSpec(memory_space=pl.ANY)
    projected = pl.pallas_call(
        kernel,
        out_shape=jax.ShapeDtypeStruct((NSEQ, 2, 8, D), BF),
        in_specs=[vmem, vmem, anywhere, anywhere],
        out_specs=anywhere,
        scratch_shapes=[
            pltpu.VMEM((NSEQ, 2, 8, D), BF),
            pltpu.VMEM((NSEQ, 2, 8, D), BF),
            pltpu.VMEM((NSEQ, QROWS, D), BF),
            pltpu.VMEM((NSEQ, OROWS, D), BF),
            pltpu.VMEM((3 * D, D), BF),
            pltpu.VMEM((D, D), BF),
            pltpu.VMEM((512, D), BF),
            pltpu.VMEM((512, D), BF),
            pltpu.VMEM((5, 4, 8, D), BF),
            pltpu.VMEM((5, 4, 8, D), BF),
            pltpu.VMEM((512, WIDE), BF),
            pltpu.VMEM((WIDE, 512), BF),
            pltpu.VMEM((512, WIDE), BF),
            pltpu.VMEM((512, D), BF),
            pltpu.VMEM((512, WIDE), BF),
            pltpu.VMEM((512, 128), BF),
            pltpu.VMEM((5, 32, WIDE), BF),
            pltpu.VMEM((5, 32, WIDE), BF),
            pltpu.VMEM((NSEQ, 2, 8, D), BF),
            pltpu.SemaphoreType.DMA((3, NSEQ)),
            pltpu.SemaphoreType.DMA((3, 2)),
            pltpu.SemaphoreType.DMA((3, 6)),
            pltpu.SemaphoreType.DMA((3, 8)),
            pltpu.SemaphoreType.DMA((3, 16)),
            pltpu.SemaphoreType.DMA((3,)),
            pltpu.SemaphoreType.DMA,
            pltpu.SemaphoreType.DMA,
            pltpu.SemaphoreType.DMA((4, 5)),
            pltpu.SemaphoreType.DMA((4, 5)),
            pltpu.SemaphoreType.DMA,
            pltpu.SemaphoreType.DMA,
        ],
        compiler_params=pltpu.CompilerParams(
            collective_id=0, has_side_effects=True, vmem_limit_bytes=60 * 2**20
        ),
    )(
        video_tokens.reshape(512, D),
        modulation.transpose(1, 0, 2),
        qkv_weight.T,
        out_weight.T,
    )
    frame_major = projected.reshape(1, 512, D)
    restored = video_tokens.astype(F32) + modulation[:, 2][:, None, :] * frame_major.astype(F32)
    return restored.astype(BF)


def solution(mesh):
    return jax.shard_map(
        per_device,
        mesh=mesh,
        in_specs=(
            P(("slab", "seq"), None, None),
            P(("slab", "seq"), None, None),
            P(None, "seq"),
            P(None, "seq"),
        ),
        out_specs=P(("slab", "seq"), None, None),
        check_vma=False,
    )
```

```python
import functools

import jax
import jax.numpy as jnp
from jax import lax
from jax.experimental import pallas as pl
from jax.experimental.pallas import tpu as pltpu
from jax.sharding import PartitionSpec as P

D = 1152
HEAD = 72
GROUP = 576
WIDE = 640
NSEQ = 32
NSLAB = 16
QROWS = 108
OROWS = 36
MESH = pl.DeviceIdType.MESH
EPS = 1e-06
BF = jnp.bfloat16
F32 = jnp.float32


def dot_nt(a, b):
    return lax.dot_general(a, b, (((1,), (1,)), ((), ())), preferred_element_type=F32)


def kernel(
    tok_ref, mod_ref, qw_ref, ow_ref, out_ref,
    hbuf, xbuf, wq, wo, wt, wot, xa, xb, halo_l, halo_u,
    qs, kts, vs, att, att_b, edge, ret_l, ret_u, obuf,
    wrecv, zsend, ysend, xsend, ssend, lsem, tsend, trecv, hsend, hrecv, osend, orecv,
):
    s = lax.axis_index("slab")
    j = lax.axis_index("seq")
    x = lax.rem(s, 4)
    zh = lax.div(s, 4)
    y = lax.div(j, 8)
    zl = lax.rem(lax.div(j, 2), 4)
    c = lax.rem(j, 2)
    even = lax.rem(x, 2) == 0
    odd = lax.rem(x, 2) == 1
    par = lax.rem(x, 2)

    def zdev(off):
        zz = lax.rem(zh * 4 + zl + off + 16, 16)
        return (lax.div(zz, 4) * 4 + x, y * 8 + lax.rem(zz, 4) * 2 + c)

    def ydev(off):
        return (s, lax.rem(y + off + 4, 4) * 8 + zl * 2 + c)

    def xdev(off):
        return (zh * 4 + lax.rem(x + off + 4, 4), j)

    sib = (s, y * 8 + zl * 2 + (1 - c))
    def rdma(src, dst, ssem, rsem_, dev):
        return pltpu.make_async_remote_copy(
            src_ref=src, dst_ref=dst, send_sem=ssem, recv_sem=rsem_,
            device_id=dev, device_id_type=MESH,
        )

    barrier = pltpu.get_barrier_semaphore()

    def greet(k, carry):
        pl.semaphore_signal(
            barrier, inc=1, device_id=(s, lax.rem(j + k, NSEQ)), device_id_type=MESH
        )
        return carry

    lax.fori_loop(1, NSEQ, greet, 0)
    for dev in (xdev(1), xdev(-1), xdev(2), zdev(1), zdev(-1), zdev(2), zdev(-2)):
        pl.semaphore_signal(barrier, inc=1, device_id=dev, device_id_type=MESH)
    for q in range(4):
        for block in (zh + 1, zh + 3):
            pl.semaphore_signal(
                barrier, inc=1, device_id=(lax.rem(block, 4) * 4 + q, j), device_id_type=MESH
            )
    own_q = pltpu.make_async_copy(qw_ref, wq.at[j], lsem.at[0])
    own_o = pltpu.make_async_copy(ow_ref, wo.at[j], lsem.at[1])
    own_q.start()
    own_o.start()

    shift = mod_ref[0]
    scale = 1.0 + mod_ref[1]

    def norm(i, carry):
        rows = pl.ds(pl.multiple_of(i * 64, 64), 64)
        values = tok_ref[rows, :].astype(F32)
        centered = values - jnp.mean(values, axis=-1, keepdims=True)
        variance = jnp.mean(centered * centered, axis=-1, keepdims=True)
        normed = centered * lax.rsqrt(variance + EPS) * scale + shift
        hbuf[pl.ds(i * 4, 4)] = normed.reshape(4, 2, 8, D).astype(BF)
        return carry

    lax.fori_loop(0, 8, norm, 0)
    own_q.wait()
    own_o.wait()
    pl.semaphore_wait(barrier, NSEQ - 1 + 15)

    def slot(yo, zo):
        return lax.rem(y + yo, 4) * 8 + lax.rem(zl + zo, 4) * 2 + c

    def part(t, q):
        if t == 2:
            return wo.at[q]
        return wq.at[q, :, pl.ds(0, 640)] if t == 0 else wq.at[q, :, pl.ds(640, 512)]

    def ship(t, q, sems, i, dev):
        rdma(part(t, q), part(t, q), sems.at[t, i], wrecv.at[t, q], dev).start()

    def shipped(t, sems, i):
        rdma(part(t, 0), part(t, 0), sems.at[t, i], wrecv.at[t, 0], sib).wait_send()

    def landed(t, q):
        rdma(part(t, q), part(t, q), zsend.at[t, 0], wrecv.at[t, q], sib).wait_recv()

    za = par * 3
    zb = 1 + par
    oa = (1 - par) * 3
    ob = 2 - par
    plus = ((0, 0), (0, 2), (1, 1), (1, 3))

    def x_ship(t, kind, yo, q):
        right = t == 0 or (t == 2 and (kind, yo) in plus)
        ship(t, q, xsend, kind * 4 + yo, xdev(1 if right else -1))

    def own_y(t):
        ship(t, j, ysend, 0, ydev(1))
        ship(t, j, ysend, 1, ydev(-1))

    def stage_z(t):
        @pl.when(even)
        def _():
            ship(t, j, zsend, 0, zdev(-1))
            if t < 2:
                own_y(t)

        @pl.when(odd)
        def _():
            ship(t, j, zsend, 0, zdev(1))

        @pl.when(odd & (zl < 3))
        def _():
            ship(t, j, zsend, 1, zdev(lax.div(zl, 2) * 4 - 2))

        ship(t, j, ssend, 0, sib)

    def stage_a(t):
        @pl.when(odd)
        def _():
            q = slot(0, za)
            landed(t, q)

            @pl.when(zl == 0)
            def _():
                ship(t, q, zsend, 2, zdev(1))

            ship(t, q, ysend, 0, ydev(1))
            ship(t, q, ysend, 1, ydev(-1))
            x_ship(t, 0, 0, q)
            ship(t, q, ssend, 1, sib)

    def stage_b(t):
        q = slot(0, zb)
        landed(t, q)
        ship(t, q, ysend, 2, ydev(1))
        ship(t, q, ysend, 3, ydev(-1))
        x_ship(t, 1, 0, q)
        ship(t, q, ssend, 2, sib)

    near = ((0, 3), (0, 1), (1, 1), (1, 3))
    far = ((0, 2), (1, 2))

    def stage_y(t, which, n):
        for kind, yo in which:
            q = slot(yo, zb if kind else za)
            landed(t, q)
            if (kind, yo) == (0, 3):
                ship(t, q, ysend, 4, ydev(1))
            if (kind, yo) == (1, 1):
                ship(t, q, ysend, 5, ydev(-1))
            x_ship(t, kind, yo, q)
            ship(t, q, ssend, n, sib)
            n += 1

    def stage_x(t):
        @pl.when(even)
        def _():
            q = slot(0, oa)
            landed(t, q)
            ship(t, q, ssend, 1, sib)

        n = 9
        for kind, yo in ((1, 0), (0, 1), (0, 3), (1, 1), (1, 3), (0, 2), (1, 2)):
            q = slot(yo, ob if kind else oa)
            landed(t, q)
            ship(t, q, ssend, n, sib)
            n += 1

    def stage_s(t):
        def other(i, carry):
            landed(t, i * 2 + 1 - c)
            return carry

        lax.fori_loop(0, 16, other, 0)

    last = lax.div(x, 3)
    first = lax.div(3 - x, 3)

    def go_up(pieces, buf, ss, rs):
        for q in range(4):
            far_slab = zh * 4 + q if q < 3 else lax.rem(zh + 1, 4) * 4
            dest = (1 - last) * (s + 1) + last * far_slab
            place = q + last * (4 - q) if q < 3 else 3
            rdma(pieces(q), buf.at[place], ss.at[q], rs.at[place], (dest, j)).start()

    def go_down(pieces, buf, ss, rs):
        for q in range(4):
            far_slab = zh * 4 + q if q > 0 else lax.rem(zh + 3, 4) * 4 + 3
            dest = (1 - first) * (s - 1) + first * far_slab
            place = q + first * (4 - q) if q > 0 else 0
            rdma(pieces(q), buf.at[place], ss.at[q], rs.at[place], (dest, j)).start()

    def pass_up(buf, ss, rs):
        @pl.when(x < 3)
        def _():
            rdma(buf.at[4], buf.at[4], ss.at[4], rs.at[4], sib).wait_recv()
            rdma(buf.at[4], buf.at[x], ss.at[4], rs.at[x], (lax.rem(zh + 1, 4) * 4, j)).start()

    def pass_down(buf, ss, rs):
        @pl.when(x > 0)
        def _():
            rdma(buf.at[4], buf.at[4], ss.at[4], rs.at[4], sib).wait_recv()
            rdma(
                buf.at[4], buf.at[x], ss.at[4], rs.at[x], (lax.rem(zh + 3, 4) * 4 + 3, j)
            ).start()

    def arrived(buf, ss, rs):
        for q in range(4):
            rdma(buf.at[q], buf.at[q], ss.at[q], rs.at[q], sib).wait_recv()

    def departed(buf, ss, rs, relayed):
        for q in range(4):
            rdma(buf.at[q], buf.at[q], ss.at[q], rs.at[q], sib).wait_send()

        @pl.when(relayed)
        def _():
            rdma(buf.at[4], buf.at[4], ss.at[4], rs.at[4], sib).wait_send()

    stage_z(0)
    stage_z(1)

    def send_tokens(yo):
        def send(k, carry):
            d = lax.rem(y + yo, 4) * 8 + lax.rem(zl * 2 + c + k, 8)
            rdma(hbuf.at[d], xbuf.at[j], tsend, trecv, (s, d)).start()
            return carry

        lax.fori_loop(0 if yo else 1, 8, send, 0)

    send_tokens(0)
    send_tokens(1)
    send_tokens(3)
    own_tok = pltpu.make_async_copy(hbuf.at[j], xbuf.at[j], lsem.at[2])
    own_tok.start()

    stage_a(0)
    stage_a(1)
    stage_b(0)
    stage_b(1)
    send_tokens(2)
    stage_y(0, near, 3)
    stage_y(1, near, 3)
    stage_z(2)
    stage_y(0, far, 7)
    stage_y(1, far, 7)

    own_tok.wait()
    rdma(xbuf.at[pl.ds(0, NSEQ - 1)], xbuf.at[pl.ds(0, NSEQ - 1)], tsend, trecv, sib).wait_recv()
    go_up(lambda q: xbuf.at[pl.ds(16 + 4 * q, 4), 0], halo_l, hsend.at[0], hrecv.at[0])
    go_down(lambda q: xbuf.at[pl.ds(4 * q, 4), 1], halo_u, hsend.at[1], hrecv.at[1])

    for b in range(2):
        rows = xbuf[:, b].astype(F32).reshape(256, D).astype(BF)
        xa[256 * b:256 * b + 256, :] = rows
    xb[128:256, :] = xa[0:128, :]
    xb[256:384, :] = xa[384:512, :]


    @pl.when(even)
    def _():
        own_y(2)

    stage_a(2)
    stage_b(2)
    stage_x(0)
    stage_x(1)
    pass_up(halo_l, hsend.at[0], hrecv.at[0])
    pass_down(halo_u, hsend.at[1], hrecv.at[1])
    stage_s(0)
    stage_s(1)
    for i in range(16):
        wt[216 * i:216 * i + 216, :] = jnp.concatenate([wq[2 * i], wq[2 * i + 1]], axis=0)
    stage_y(2, near, 3)

    def project(g, rows_ref):
        base = 1728 * g
        vbase = 2816 if g else 1152
        rows = rows_ref[...]
        qs[...] = dot_nt(rows, wt[base:base + WIDE, :]).astype(BF)
        kts[...] = dot_nt(wt[base + GROUP:base + GROUP + WIDE, :], rows).astype(BF)
        vs[...] = dot_nt(rows, wt[vbase:vbase + WIDE, :]).astype(BF)

    def attend(g, store):
        phase = 64 * g
        row_id = lax.broadcasted_iota(jnp.int32, (256, 256), 0)
        col_id = lax.broadcasted_iota(jnp.int32, (256, 256), 1)
        same = lax.rem(row_id, 8) == lax.rem(col_id, 8)

        def block(b, carry):
            at = pl.ds(pl.multiple_of(b * 256, 256), 256)
            tiles = {}
            for h in range(8):
                lo = HEAD * h
                t0, t1 = lo // 128, (lo + HEAD - 1) // 128
                width = 128 * (t1 - t0 + 1)
                r = lax.broadcasted_iota(jnp.int32, (width, 256), 0) + t0 * 128
                keep = jnp.where((r >= lo) & (r < lo + HEAD), 1.0, 0.0).astype(BF)
                kt = kts[t0 * 128:t0 * 128 + width, at] * keep
                scores = jnp.dot(
                    qs[at, t0 * 128:t0 * 128 + width], kt, preferred_element_type=F32
                ) * (HEAD ** -0.5)
                scores = jnp.where(same, scores, -1e30)
                top = jnp.max(scores, axis=-1, keepdims=True)
                e = jnp.exp(scores - top)
                p = (e * (1.0 / jnp.sum(e, axis=-1, keepdims=True))).astype(BF)
                lo = HEAD * h + phase
                t0, t1 = lo // 128, (lo + HEAD - 1) // 128
                width = 128 * (t1 - t0 + 1)
                r = lax.broadcasted_iota(jnp.int32, (256, width), 1) + t0 * 128
                keep = jnp.where((r >= lo) & (r < lo + HEAD), 1.0, 0.0).astype(BF)
                v = vs[at, t0 * 128:t0 * 128 + width] * keep
                o = jnp.dot(p, v, preferred_element_type=F32)
                for t in range(t0, t1 + 1):
                    piece = o[:, (t - t0) * 128:(t - t0 + 1) * 128]
                    tiles[t] = tiles[t] + piece if t in tiles else piece
                for t in list(tiles):
                    if h == 7 or t < (HEAD * (h + 1) + phase) // 128:
                        store(at, t, tiles.pop(t).astype(BF))
            return carry

        lax.fori_loop(0, 2, block, 0)

    def store_a(at, t, value):
        if t < 4:
            att[at, t * 128:t * 128 + 128] = value
        else:
            edge[at, :] = value

    def store_b(at, t, value):
        att_b[at, t * 128:t * 128 + 128] = value

    project(0, xa)
    attend(0, store_a)
    stage_y(2, far, 7)
    arrived(halo_l, hsend.at[0], hrecv.at[0])
    arrived(halo_u, hsend.at[1], hrecv.at[1])
    xb[0:128, :] = halo_l[0:4].astype(F32).reshape(128, D).astype(BF)
    xb[384:512, :] = halo_u[0:4].astype(F32).reshape(128, D).astype(BF)
    project(1, xb)
    stage_x(2)
    attend(1, store_b)

    go_down(lambda q: att_b.at[pl.ds(32 * q, 32)], ret_l, hsend.at[2], hrecv.at[2])
    go_up(lambda q: att_b.at[pl.ds(384 + 32 * q, 32)], ret_u, hsend.at[3], hrecv.at[3])

    stage_s(2)
    for i in range(16):
        wot[72 * i:72 * i + 72, :] = jnp.concatenate([wo[2 * i], wo[2 * i + 1]], axis=0)

    def finish(rows, part):
        att[rows, 512:640] = edge[rows, :] + part[:, 0:128]
        att[rows, 640:1152] = part[:, 128:640]
        return dot_nt(att[rows, :], wot[...]).reshape(16, 8, D).astype(BF)

    def send_half(low, high, steps):
        for yo in steps:
            def send_out(k, carry, yo=yo):
                d = lax.rem(y + yo, 4) * 8 + lax.rem(zl * 2 + c + k, 8)
                b = lax.div(d, 16) * (high - low) + low
                rdma(obuf.at[d, b], out_ref.at[j, b], osend, orecv, (s, d)).start()
                return carry

            lax.fori_loop(0 if yo else 1, 8, send_out, 0)

    obuf[0:16, 0] = finish(slice(0, 128), att_b[128:256, :])
    obuf[16:32, 1] = finish(slice(384, 512), att_b[256:384, :])
    send_half(0, 1, (0,))
    pass_down(ret_l, hsend.at[2], hrecv.at[2])
    pass_up(ret_u, hsend.at[3], hrecv.at[3])
    send_half(0, 1, (2, 1, 3))
    arrived(ret_l, hsend.at[2], hrecv.at[2])
    obuf[16:32, 0] = finish(slice(128, 256), ret_l[0:4].reshape(128, WIDE))
    arrived(ret_u, hsend.at[3], hrecv.at[3])
    obuf[0:16, 1] = finish(slice(256, 384), ret_u[0:4].reshape(128, WIDE))
    send_half(1, 0, (2, 1, 3, 0))
    own_out = pltpu.make_async_copy(obuf.at[j], out_ref.at[j], lsem.at[2])
    own_out.start()

    for t in range(3):
        shipped(t, zsend, 0)

        @pl.when(odd)
        def _():
            shipped(t, xsend, 0)

        @pl.when(odd & (zl < 3))
        def _():
            shipped(t, zsend, 1)

        @pl.when(odd & (zl == 0))
        def _():
            shipped(t, zsend, 2)

        for i in range(6):
            shipped(t, ysend, i)
        for i in range(1, 8):
            shipped(t, xsend, i)
        for i in range(16):
            shipped(t, ssend, i)
    departed(halo_l, hsend.at[0], hrecv.at[0], x < 3)
    departed(halo_u, hsend.at[1], hrecv.at[1], x > 0)
    departed(ret_l, hsend.at[2], hrecv.at[2], x > 0)
    departed(ret_u, hsend.at[3], hrecv.at[3], x < 3)
    own_out.wait()
    many = pl.ds(0, NSEQ - 1)
    rdma(hbuf.at[many], xbuf.at[many], tsend, trecv, sib).wait_send()
    rdma(obuf.at[many], out_ref.at[many], osend, orecv, sib).wait_send()
    rdma(obuf.at[many], out_ref.at[many], osend, orecv, sib).wait_recv()


def per_device(video_tokens, modulation, qkv_weight, out_weight):
    vmem = pl.BlockSpec(memory_space=pltpu.VMEM)
    anywhere = pl.BlockSpec(memory_space=pl.ANY)
    projected = pl.pallas_call(
        kernel,
        out_shape=jax.ShapeDtypeStruct((NSEQ, 2, 8, D), BF),
        in_specs=[vmem, vmem, anywhere, anywhere],
        out_specs=anywhere,
        scratch_shapes=[
            pltpu.VMEM((NSEQ, 2, 8, D), BF),
            pltpu.VMEM((NSEQ, 2, 8, D), BF),
            pltpu.VMEM((NSEQ, QROWS, D), BF),
            pltpu.VMEM((NSEQ, OROWS, D), BF),
            pltpu.VMEM((3 * D, D), BF),
            pltpu.VMEM((D, D), BF),
            pltpu.VMEM((512, D), BF),
            pltpu.VMEM((512, D), BF),
            pltpu.VMEM((5, 4, 8, D), BF),
            pltpu.VMEM((5, 4, 8, D), BF),
            pltpu.VMEM((512, WIDE), BF),
            pltpu.VMEM((WIDE, 512), BF),
            pltpu.VMEM((512, WIDE), BF),
            pltpu.VMEM((512, D), BF),
            pltpu.VMEM((512, WIDE), BF),
            pltpu.VMEM((512, 128), BF),
            pltpu.VMEM((5, 32, WIDE), BF),
            pltpu.VMEM((5, 32, WIDE), BF),
            pltpu.VMEM((NSEQ, 2, 8, D), BF),
            pltpu.SemaphoreType.DMA((3, NSEQ)),
            pltpu.SemaphoreType.DMA((3, 3)),
            pltpu.SemaphoreType.DMA((3, 6)),
            pltpu.SemaphoreType.DMA((3, 8)),
            pltpu.SemaphoreType.DMA((3, 16)),
            pltpu.SemaphoreType.DMA((3,)),
            pltpu.SemaphoreType.DMA,
            pltpu.SemaphoreType.DMA,
            pltpu.SemaphoreType.DMA((4, 5)),
            pltpu.SemaphoreType.DMA((4, 5)),
            pltpu.SemaphoreType.DMA,
            pltpu.SemaphoreType.DMA,
        ],
        compiler_params=pltpu.CompilerParams(
            collective_id=0, has_side_effects=True, vmem_limit_bytes=60 * 2**20
        ),
    )(
        video_tokens.reshape(512, D),
        modulation.transpose(1, 0, 2),
        qkv_weight.T,
        out_weight.T,
    )
    frame_major = projected.reshape(1, 512, D)
    restored = video_tokens.astype(F32) + modulation[:, 2][:, None, :] * frame_major.astype(F32)
    return restored.astype(BF)


def solution(mesh):
    return jax.shard_map(
        per_device,
        mesh=mesh,
        in_specs=(
            P(("slab", "seq"), None, None),
            P(("slab", "seq"), None, None),
            P(None, "seq"),
            P(None, "seq"),
        ),
        out_specs=P(("slab", "seq"), None, None),
        check_vma=False,
    )
```
